512 devices in a mesh: grp: 16 (over y, x), tile: 32 (over z, core).
Axes of the slice: x: 4, y: 4, z: 16, core: 2. Of those that a mesh axis runs over, the one named last changes fastest.
Arguments:
- features: bfloat16 [131072, 128], P(('grp', 'tile')), may hold values from -6 to 6
- source_rows: int32 [27, 1024, 128], P(None, ('grp', 'tile')), may hold values from -1 to 127, as said below
- target_codes: int32 [27, 1024], P(None, ('grp', 'tile')), may hold values from 0 to 5, as said below
- block_count: int32 [512], P(('grp', 'tile')), may hold values from 1 to 2, as said below
- weight_one: bfloat16 [27, 128, 128], replicated, may hold values from -0.125 to 0.125
- weight_two: bfloat16 [27, 128, 128], replicated, may hold values from -0.125 to 0.125
- out_cotangent: bfloat16 [131072, 128], P(('grp', 'tile')), may hold values from -6 to 6
Outputs:
- block_out: bfloat16 [131072, 128], P(('grp', 'tile'))
- input_grad: bfloat16 [131072, 128], P(('grp', 'tile'))
- wgrad_one: float32 [3456, 128], P('grp')
- wgrad_two: float32 [3456, 128], P('grp')
The draws below stay inside these ranges and needn't reach their ends.
Inputs may be any that keep to these rules, and one draw needn't show every extreme that they name: `source_rows`: entry [k, j, r] is the row of source block j that reaches row r of its target block under offset k, or -1 for none. `target_codes`: a code s * 2 + b names block b of tile t - 1 + s of the same group, t being the source block's tile; offset k = 9 (dx + 1) + 3 (dy + 1) + (dz + 1); s = 1 except s = 0 for offsets with dz = -1 from block 0 of a tile, and s = 2 for offsets with dz = +1 from the last active block of a tile. Blocks of a tile from block_count on are empty.
All inputs are finite; a program needn't handle non-finite values.
Results may differ from the reference program's by a relative error of at most 0.025.
Values may be sent and summed in bfloat16 or wider, within the bound.
A program may use at most 64 MiB of HBM per device.

```python
import jax
import jax.numpy as jnp
from jax import lax

C = 128
KVOL = 27
BLK = 128
NB = 2
TILES = 512
BLOCKS = 1024
VOXELS = 131072
N_GRP = 16
N_TILE = 32


def shared_counts(key):
    return jax.random.randint(jax.random.fold_in(key, 7), (TILES,), 1, NB + 1).astype(jnp.int32)


def draw_block_count(key, part):
    return shared_counts(key)


def draw_target_codes(key, part):
    counts = shared_counts(key)
    target_block = jax.random.randint(jax.random.fold_in(key, 11), (KVOL, BLOCKS), 0, NB).astype(jnp.int32)
    offset_index = jnp.arange(KVOL, dtype=jnp.int32)[:, None]
    block_index = jnp.arange(BLOCKS, dtype=jnp.int32)[None, :]
    within = block_index % NB
    last_active = counts[block_index // NB] - 1
    lower = (offset_index % 3 == 0) & (within == 0)
    upper = (offset_index % 3 == 2) & (within == last_active)
    side = 1 - lower.astype(jnp.int32) + upper.astype(jnp.int32)
    return (side * NB + target_block).astype(jnp.int32)


def draw_source_rows(key, part):
    first, second = jax.random.split(key)
    picked = jax.random.randint(first, (KVOL, BLOCKS, BLK), 0, BLK)
    keeper = jax.random.randint(second, (KVOL, BLOCKS, BLK), 0, 2)
    return jnp.where(keeper == 1, picked, -1).astype(jnp.int32)


def block_scale(rng, extent, cuts, smallest, high):
    gain, own = 1.0, jax.random.fold_in(rng, 6)
    for position, blocks in cuts:
        steps = jnp.exp(jax.random.uniform(jax.random.fold_in(own, position), (blocks,), jnp.float32, smallest / len(cuts), high / len(cuts)))
        gain = gain * jnp.repeat(steps, extent[position] // blocks).reshape([-1 if axis == position else 1 for axis in range(len(extent))])
    return gain


def centred(stream_key, shape, spread, reach, shards=(), kind=jnp.bfloat16):
    loudness = block_scale(stream_key, shape, shards, -0.22, 0.18) if shards else 1.0
    values = jax.random.normal(stream_key, shape, jnp.float32) * spread * loudness
    return jnp.minimum(jnp.maximum(values, -reach), reach).astype(kind)


def setup_inputs(seed: int = 0) -> dict:
    seeds = jax.random.split(jax.random.key(seed), 8)
    features = centred(seeds[0], (VOXELS, C), 1.0, 6.0, ((0, 512),))
    source_rows = draw_source_rows(jax.random.fold_in(seeds[7], 71), 0)
    target_codes = draw_target_codes(jax.random.fold_in(seeds[7], 71), 0)
    block_count = draw_block_count(jax.random.fold_in(seeds[7], 71), 0)
    weight_one = centred(seeds[4], (KVOL, C, C), (14 * C) ** -0.5, 0.125)
    weight_two = centred(seeds[5], (KVOL, C, C), (14 * C) ** -0.5, 0.125)
    out_cotangent = centred(seeds[6], (VOXELS, C), 1.0, 6.0, ((0, 512),))
    return dict(features=features, source_rows=source_rows, target_codes=target_codes, block_count=block_count, weight_one=weight_one, weight_two=weight_two, out_cotangent=out_cotangent)


def silu_grad(values):
    sigma = jax.nn.sigmoid(values)
    return sigma * (1.0 + values * (1.0 - sigma))

def tile_gather(field, row_map, active):
    offsets, blocks_dev, block_rows = row_map.shape
    valid_rows = (row_map >= 0) & active[None, :, None]
    flat_rows = (jnp.arange(blocks_dev, dtype=jnp.int32)[None, :, None] * block_rows + jnp.maximum(row_map, 0)).astype(jnp.int32).reshape(-1)
    picked = jnp.take(field, flat_rows, axis=0).reshape(offsets, blocks_dev * block_rows, -1)
    valid_mask = valid_rows.reshape(offsets, blocks_dev * block_rows, 1)
    picked = jnp.where(valid_mask, picked, jnp.zeros_like(picked))
    return (picked, flat_rows, valid_mask)

def tile_spread(picked, weights, codes):
    offsets, total_rows, channels = picked.shape
    blocks_dev = codes.shape[1]
    block_rows = total_rows // blocks_dev
    partial_value = jnp.einsum('kmc,kcd->kmd', picked.astype(jnp.float32), weights.astype(jnp.float32), precision=lax.Precision.HIGHEST)
    one_hot = (codes[:, :, None] == jnp.arange(3 * blocks_dev, dtype=jnp.int32)[None, None, :]).astype(jnp.float32)
    buffer = jnp.einsum('kis,kirc->src', one_hot, partial_value.reshape(offsets, blocks_dev, block_rows, -1), precision=lax.Precision.HIGHEST)
    return buffer.reshape(3, blocks_dev * block_rows, -1)

def tile_pull(stacked, codes, picked, flat_rows, valid_mask, weights):
    offsets, total_rows, channels = picked.shape
    blocks_dev = codes.shape[1]
    grid_blocks = stacked.reshape(3 * blocks_dev, total_rows // blocks_dev, -1)
    grad_rows = jnp.take(grid_blocks, codes.reshape(-1).astype(jnp.int32), axis=0).reshape(offsets, total_rows, -1)
    wgrad = jnp.einsum('kmc,kmd->kcd', picked.astype(jnp.float32), grad_rows.astype(jnp.float32), precision=lax.Precision.HIGHEST)
    grad_pick = jnp.einsum('kmd,kcd->kmc', grad_rows.astype(jnp.float32), weights.astype(jnp.float32), precision=lax.Precision.HIGHEST)
    grad_pick = jnp.where(valid_mask, grad_pick, jnp.zeros_like(grad_pick))
    grad_in = jnp.zeros((total_rows, channels), jnp.float32).at[flat_rows].add(grad_pick.reshape(-1, channels))
    return (wgrad, grad_in)

def join_partials(buffer):
    zero_tile = jnp.zeros_like(buffer[:1, 0])
    from_next = jnp.concatenate([buffer[1:, 0], zero_tile], axis=0)
    from_prev = jnp.concatenate([zero_tile, buffer[:-1, 2]], axis=0)
    return buffer[:, 1] + from_next + from_prev

def neighbor_rows(grads):
    zero_tile = jnp.zeros_like(grads[:1])
    before = jnp.concatenate([zero_tile, grads[:-1]], axis=0)
    after = jnp.concatenate([grads[1:], zero_tile], axis=0)
    return jnp.concatenate([before, grads, after], axis=1)

def group_pass(feature_grid, row_maps, code_grid, count_grid, cotangent, weight_one, weight_two):
    blocks_dev = code_grid.shape[2]
    block_rows = row_maps.shape[3]
    active = jnp.arange(blocks_dev, dtype=jnp.int32)[None, :] < count_grid[:, None]
    row_mask = jnp.repeat(active, block_rows, axis=1).astype(jnp.float32)[:, :, None]
    pick_in, flat_rows, valid_mask = jax.vmap(tile_gather)(feature_grid, row_maps, active)
    pre_one = join_partials(jax.vmap(lambda p, c: tile_spread(p, weight_one, c))(pick_in, code_grid))
    hidden = (jax.nn.silu(pre_one) * row_mask).astype(jnp.bfloat16)
    pick_mid = jax.vmap(lambda h, r, a: tile_gather(h, r, a)[0])(hidden, row_maps, active)
    total = join_partials(jax.vmap(lambda p, c: tile_spread(p, weight_two, c))(pick_mid, code_grid)) + feature_grid.astype(jnp.float32)
    result = (jax.nn.silu(total) * row_mask).astype(jnp.bfloat16)
    grad_sum = (cotangent.astype(jnp.float32) * silu_grad(total) * row_mask).astype(jnp.bfloat16)
    wgrad_two, grad_mid = jax.vmap(lambda s, c, p, f, v: tile_pull(s, c, p, f, v, weight_two))(neighbor_rows(grad_sum), code_grid, pick_mid, flat_rows, valid_mask)
    grad_pre = (grad_mid * silu_grad(pre_one) * row_mask).astype(jnp.bfloat16)
    wgrad_one, grad_conv = jax.vmap(lambda s, c, p, f, v: tile_pull(s, c, p, f, v, weight_one))(neighbor_rows(grad_pre), code_grid, pick_in, flat_rows, valid_mask)
    input_grad = (grad_conv + grad_sum.astype(jnp.float32)).astype(jnp.bfloat16)
    return (result, input_grad, lax.optimization_barrier(jnp.sum(wgrad_one, axis=0)), lax.optimization_barrier(jnp.sum(wgrad_two, axis=0)))

def reference(features, source_rows, target_codes, block_count, weight_one, weight_two, out_cotangent):
    groups = N_GRP
    tiles = N_TILE
    feature_grid = features.reshape(groups, tiles, NB * BLK, C)
    row_maps = source_rows.reshape(KVOL, groups, tiles, NB, BLK).transpose(1, 2, 0, 3, 4)
    code_grid = target_codes.reshape(KVOL, groups, tiles, NB).transpose(1, 2, 0, 3)
    count_grid = block_count.reshape(groups, tiles)
    cotangent = out_cotangent.reshape(groups, tiles, NB * BLK, C)
    result, input_grad, sums_one, sums_two = lax.map(lambda a: group_pass(a[0], a[1], a[2], a[3], a[4], weight_one, weight_two), (feature_grid, row_maps, code_grid, count_grid, cotangent))
    scale = float(VOXELS) ** (-0.5)
    wgrad_one = (lax.optimization_barrier(jnp.sum(sums_one, axis=0)) * scale).reshape(KVOL * C, C)
    wgrad_two = (lax.optimization_barrier(jnp.sum(sums_two, axis=0)) * scale).reshape(KVOL * C, C)
    return (result.reshape(VOXELS, C), input_grad.reshape(VOXELS, C), wgrad_one, wgrad_two)
```

```python
import functools
import math

import jax
import jax.numpy as jnp
from jax import lax
from jax.experimental import pallas as pl
from jax.experimental.pallas import tpu as pltpu
from jax.sharding import PartitionSpec as P

MESH = pl.DeviceIdType.MESH
BF = jnp.bfloat16
F32 = jnp.float32
I32 = jnp.int32


def nn(a, b):
    return lax.dot_general(a, b, (((1,), (0,)), ((), ())), preferred_element_type=F32)


def nt(a, b):
    return lax.dot_general(a, b, (((1,), (1,)), ((), ())), preferred_element_type=F32)


def silu_parts(v):
    s = 1.0 / (1.0 + jnp.exp(-v))
    return v * s, s * (1.0 + v * (1.0 - s))


def kernel(
    dims,
    feat,
    src,
    codes,
    count,
    w_one,
    w_two,
    cot,
    out_ref,
    dx_ref,
    wg_one,
    wg_two,
    ot,
    pt,
    gt,
    wraw,
    wt,
    wc,
    ht,
    hid,
    pre,
    q,
    xs,
    xr,
    qe,
    wgf,
    cs,
    cr,
    sx,
    rx,
    ab,
    bb,
    fb,
    w_sem,
    x_send,
    x_recv,
    c_send,
    c_recv,
    g_send,
    g_recv,
    a_send,
    a_recv,
    b_send,
    b_recv,
    f_send,
    f_recv,
):
    n_grp, n_tile, kvol, rows_k, side, zside = dims
    third = kvol // 3
    B = rows_k
    shard = kvol * B // n_grp
    half = cs.shape[2]
    g = lax.axis_index("grp")
    t = lax.axis_index("tile")
    nz = n_tile // 2
    z = t // 2
    core = t % 2
    gy = g // side
    gx = g % side
    left = lax.rem(t + n_tile - 1, n_tile)
    right = lax.rem(t + 1, n_tile)
    sib = t + 1 - 2 * core
    zlo = z % zside
    zhi = z // zside

    def grp_of(o):
        dy, dx = o // side, o % side
        return lax.rem(gy + dy, side) * side + lax.rem(gx + dx, side)

    def near_z(d):
        return (zhi * zside + lax.rem(zlo + d, zside)) * 2 + core

    def far_z(d):
        return (lax.rem(zhi + d, zside) * zside + zlo) * 2 + core

    for k, w in ((0, w_one), (1, w_two)):
        pltpu.make_async_copy(w, wraw.at[k], w_sem.at[k]).start()

    barrier = pltpu.get_barrier_semaphore()
    partners = [{"tile": left}, {"tile": right}]
    partners += [{"grp": grp_of(o)} for o in range(1, n_grp)]
    partners += [{"tile": near_z(d)} for d in range(1, zside)]
    partners += [{"tile": far_z(d)} for d in range(1, zside)]
    for p in partners:
        pl.semaphore_signal(barrier, inc=1, device_id=p, device_id_type=MESH)

    two = count[0] - 1
    two_f = two.astype(F32)
    one_f = 1.0 - two_f
    keep_prev = jnp.where(t == 0, 0.0, 1.0)
    keep_next = jnp.where(t == n_tile - 1, 0.0, 1.0)

    for j in range(2):
        ht[:, j * B : (j + 1) * B] = feat[j * B : (j + 1) * B, :].T

    iota = lax.broadcasted_iota(I32, (B, B), 0)

    def onehot(k, carry):
        for j in range(2):
            row = src[k, pl.ds(j, 1), :]
            high = codes[k, j] & 1
            live = two if j else 1
            for b in range(2):
                m = (high if b else 1 - high) * live
                idx = row * m + (m - 1)
                hit = jnp.where(iota == idx, 1.0, 0.0).astype(BF)
                ot[k, j * B : (j + 1) * B, b * B : (b + 1) * B] = hit
        return carry

    lax.fori_loop(0, kvol, onehot, 0)

    def prep(w):
        pltpu.make_async_copy(w_two if w else w_one, wraw.at[w], w_sem.at[w]).wait()

        def body(i, carry):
            for pos, cls in enumerate((1, 0, 2)):
                at = pl.multiple_of((pos * third + i) * B, B)
                block = wraw[w, 3 * i + cls]
                wc[w, :, pl.ds(at, B)] = block
                wt[w, :, pl.ds(at, B)] = block.T
            return carry

        lax.fori_loop(0, third, body, 0)

    n1 = third * B

    def put(slot, i, value):
        at = pl.multiple_of((slot * third + i) * B, B)
        pt[pl.ds(at, B), :] = value.astype(BF)

    def forward_edges(field, w):
        def body(i, carry):
            put(2, i, nn(field[:, :B], ot[3 * i, :B, :]))
            put(3, i, nn(field[:, :B], ot[3 * i + 2, :B, :]))
            put(4, i, nn(field[:, B:], ot[3 * i + 2, B:, :]))
            return carry

        lax.fori_loop(0, third, body, 0)
        to_prev = nn(wt[w, :, n1 : 2 * n1], pt[2 * n1 : 3 * n1, :])
        part_a = nn(wt[w, :, 2 * n1 :], pt[3 * n1 : 4 * n1, :])
        part_b = nn(wt[w, :, 2 * n1 :], pt[4 * n1 :, :])
        xs[w, 0] = to_prev.astype(BF)
        xs[w, 1] = (part_b + part_a * one_f).astype(BF)
        return part_a * two_f

    def forward_own(field, w):
        def body(i, carry):
            put(0, i, nn(field[...], ot[3 * i + 1]))
            put(1, i, nn(field[:, B:], ot[3 * i, B:, :]))
            return carry

        lax.fori_loop(0, third, body, 0)
        return nn(wt[w, :, : 2 * n1], pt[: 2 * n1, :])

    def exchange(e, to_prev, to_next):
        return [
            pltpu.make_async_remote_copy(
                src_ref=to_prev,
                dst_ref=xr.at[e, 1],
                send_sem=x_send.at[e, 1],
                recv_sem=x_recv.at[e, 1],
                device_id={"tile": left},
                device_id_type=MESH,
            ),
            pltpu.make_async_remote_copy(
                src_ref=to_next,
                dst_ref=xr.at[e, 0],
                send_sem=x_send.at[e, 0],
                recv_sem=x_recv.at[e, 0],
                device_id={"tile": right},
                device_id_type=MESH,
            ),
        ]

    def from_sides(e):
        return (
            xr[e, 0].astype(F32) * keep_prev,
            xr[e, 1].astype(F32) * keep_next,
        )

    def start(copies):
        for c in copies:
            c.start()
        return copies

    def landed(copies):
        for c in copies:
            c.wait_recv()

    pending = []
    mask = jnp.where(
        lax.broadcasted_iota(I32, (1, 2 * B), 1) < B * count[0], 1.0, 0.0
    )

    prep(0)
    extra = forward_edges(ht, 0)
    pl.semaphore_wait(barrier, len(partners))
    moved = start(exchange(0, xs.at[0, 0], xs.at[0, 1]))
    pending += moved
    own = forward_own(ht, 0) + extra
    prep(1)
    landed(moved)
    before, after = from_sides(0)
    pre_one = own + before + after
    pre[...] = pre_one
    hid[...] = (silu_parts(pre_one)[0] * mask).astype(BF)

    extra = forward_edges(hid, 1)
    moved = start(exchange(1, xs.at[1, 0], xs.at[1, 1]))
    pending += moved
    own = forward_own(hid, 1) + extra + ht[...].astype(F32)
    cot_t = jnp.concatenate(
        [cot[:B, :].astype(F32).T, cot[B:, :].astype(F32).T], axis=1
    )
    landed(moved)
    before, after = from_sides(1)
    total = own + before + after
    value, slope = silu_parts(total)
    q[1] = (cot_t * slope * mask).astype(BF)
    moved = start(exchange(2, q.at[1], q.at[1]))
    pending += moved
    result = value * mask
    for j in range(2):
        out_ref[j * B : (j + 1) * B, :] = result[:, j * B : (j + 1) * B].T.astype(BF)

    def put_g(pos, i, lo, hi, v):
        at = pl.multiple_of((pos * third + i) * B, B)
        gt[pl.ds(at, B), lo:hi] = v.astype(BF)

    def back_own(w):
        def body(i, carry):
            put_g(0, i, 0, 2 * B, nt(q[w], ot[3 * i + 1]))
            put_g(1, i, B, 2 * B, nt(q[w], ot[3 * i, B:, :]))
            return carry

        lax.fori_loop(0, third, body, 0)

    def back_edges(w, e):
        before, after = from_sides(e)
        mixed = (after * one_f + q[w].astype(F32) * two_f).astype(BF)
        before = before.astype(BF)
        after = after.astype(BF)
        qe[0] = before
        qe[1] = mixed
        qe[2] = after

        def body(i, carry):
            put_g(1, i, 0, B, nt(qe[0], ot[3 * i, :B, :]))
            put_g(2, i, 0, B, nt(qe[1], ot[3 * i + 2, :B, :]))
            put_g(2, i, B, 2 * B, nt(qe[2], ot[3 * i + 2, B:, :]))
            return carry

        lax.fori_loop(0, third, body, 0)

    def weight_grads(field, w):
        def body(i, carry):
            for pos, cls in enumerate((1, 0, 2)):
                at = pl.multiple_of((pos * third + i) * B, B)
                to = pl.multiple_of((3 * i + cls) * B, B)
                wgf[w, pl.ds(to, B), :] = nt(field[...], gt[pl.ds(at, B), :])
            return carry

        lax.fori_loop(0, third, body, 0)

    def half_rows(w, s, h):
        at = pl.multiple_of(s * shard + h * half, 8)
        return wgf[w, pl.ds(at, half), :]

    def send_pair(w):
        def body(s, carry):
            cs[w, s] = half_rows(w, s, 1 - core).astype(BF)
            return carry

        lax.fori_loop(0, n_grp, body, 0)
        return start(
            [
                pltpu.make_async_remote_copy(
                    src_ref=cs.at[w],
                    dst_ref=cr.at[w],
                    send_sem=c_send.at[w],
                    recv_sem=c_recv.at[w],
                    device_id={"tile": sib},
                    device_id_type=MESH,
                )
            ]
        )

    def send_plane(w, moved):
        landed(moved)

        def body(s, carry):
            sx[w, s] = (half_rows(w, s, core) + cr[w, s].astype(F32)).astype(BF)
            return carry

        lax.fori_loop(0, n_grp, body, 0)
        return start(
            [
                pltpu.make_async_remote_copy(
                    src_ref=sx.at[w, grp_of(o)],
                    dst_ref=rx.at[w, o],
                    send_sem=g_send.at[w, o],
                    recv_sem=g_recv.at[w, o],
                    device_id={"grp": grp_of(o)},
                    device_id_type=MESH,
                )
                for o in range(1, n_grp)
            ]
        )

    def send_near(w, moved):
        landed(moved)
        acc = sx[w, g].astype(F32)
        for o in range(1, n_grp):
            acc = acc + rx[w, o].astype(F32)
        ab[w, zlo] = acc.astype(BF)
        return start(
            [
                pltpu.make_async_remote_copy(
                    src_ref=ab.at[w, zlo],
                    dst_ref=ab.at[w, zlo],
                    send_sem=a_send.at[w, d],
                    recv_sem=a_recv.at[w, d],
                    device_id={"tile": near_z(d)},
                    device_id_type=MESH,
                )
                for d in range(1, zside)
            ]
        )

    def send_far(w, moved):
        landed(moved)
        acc = ab[w, 0].astype(F32)
        for d in range(1, zside):
            acc = acc + ab[w, d].astype(F32)
        bb[w, zhi] = acc.astype(BF)
        return start(
            [
                pltpu.make_async_remote_copy(
                    src_ref=bb.at[w, zhi],
                    dst_ref=bb.at[w, zhi],
                    send_sem=b_send.at[w, d],
                    recv_sem=b_recv.at[w, d],
                    device_id={"tile": far_z(d)},
                    device_id_type=MESH,
                )
                for d in range(1, zside)
            ]
        )

    def send_last(w, moved):
        landed(moved)
        acc = bb[w, 0].astype(F32)
        for d in range(1, zside):
            acc = acc + bb[w, d].astype(F32)
        fb[w, core] = acc
        return start(
            [
                pltpu.make_async_remote_copy(
                    src_ref=fb.at[w, core],
                    dst_ref=fb.at[w, core],
                    send_sem=f_send.at[w],
                    recv_sem=f_recv.at[w],
                    device_id={"tile": sib},
                    device_id_type=MESH,
                )
            ]
        )

    scale = float(n_grp * n_tile * 2 * B) ** (-0.5)

    def finish(w, moved):
        landed(moved)
        dst = wg_two if w else wg_one
        dst[:half, :] = fb[w, 0] * scale
        dst[half:, :] = fb[w, 1, : shard - half, :] * scale

    for w in range(2 if wgf.shape[1] > kvol * B else 0):
        wgf[w, kvol * B :, :] = jnp.zeros((wgf.shape[1] - kvol * B, B), F32)

    back_own(1)
    landed(moved)
    back_edges(1, 2)
    grad_mid = nn(wc[1], gt[...])
    slope = silu_parts(pre[...])[1]
    q[0] = (grad_mid * slope * mask).astype(BF)
    moved = start(exchange(3, q.at[0], q.at[0]))
    pending += moved
    weight_grads(hid, 1)
    pair_two = send_pair(1)
    back_own(0)
    plane_two = send_plane(1, pair_two)
    landed(moved)
    back_edges(0, 3)
    weight_grads(ht, 0)
    pair_one = send_pair(0)
    grad_in = nn(wc[0], gt[...]) + q[1].astype(F32)
    plane_one = send_plane(0, pair_one)
    for j in range(2):
        dx_ref[j * B : (j + 1) * B, :] = grad_in[:, j * B : (j + 1) * B].T.astype(BF)
    near_two = send_near(1, plane_two)
    near_one = send_near(0, plane_one)
    far_two = send_far(1, near_two)
    far_one = send_far(0, near_one)
    last_two = send_last(1, far_two)
    finish(1, last_two)
    last_one = send_last(0, far_one)
    finish(0, last_one)
    pending += pair_two + plane_two + pair_one + plane_one
    pending += near_two + near_one + far_two + far_one + last_two + last_one
    for c in pending:
        c.wait_send()


def on_device(n_grp, n_tile, features, source_rows, target_codes, block_count, w1, w2, cot):
    kvol, _, B = source_rows.shape
    side = math.isqrt(n_grp)
    zside = math.isqrt(n_tile // 2)
    shard = kvol * B // n_grp
    half = -(-shard // 32) * 16
    wide = kvol * B
    vmem = pl.BlockSpec(memory_space=pltpu.VMEM)
    smem = pl.BlockSpec(memory_space=pltpu.SMEM)
    hbm = pl.BlockSpec(memory_space=pl.ANY)
    dma = pltpu.SemaphoreType.DMA
    dims = (n_grp, n_tile, kvol, B, side, zside)
    return pl.pallas_call(
        functools.partial(kernel, dims),
        out_shape=(
            jax.ShapeDtypeStruct((2 * B, B), BF),
            jax.ShapeDtypeStruct((2 * B, B), BF),
            jax.ShapeDtypeStruct((shard, B), F32),
            jax.ShapeDtypeStruct((shard, B), F32),
        ),
        in_specs=[vmem, vmem, smem, smem, hbm, hbm, vmem],
        out_specs=(vmem,) * 4,
        scratch_shapes=[
            pltpu.VMEM((kvol, 2 * B, 2 * B), BF),
            pltpu.VMEM((5 * (kvol // 3) * B, 2 * B), BF),
            pltpu.VMEM((wide, 2 * B), BF),
            pltpu.VMEM((2, kvol, B, B), BF),
            pltpu.VMEM((2, B, wide), BF),
            pltpu.VMEM((2, B, wide), BF),
            pltpu.VMEM((B, 2 * B), BF),
            pltpu.VMEM((B, 2 * B), BF),
            pltpu.VMEM((B, 2 * B), F32),
            pltpu.VMEM((2, B, 2 * B), BF),
            pltpu.VMEM((2, 2, B, 2 * B), BF),
            pltpu.VMEM((4, 2, B, 2 * B), BF),
            pltpu.VMEM((3, B, 2 * B), BF),
            pltpu.VMEM((2, wide + 2 * half - shard, B), F32),
            pltpu.VMEM((2, n_grp, half, B), BF),
            pltpu.VMEM((2, n_grp, half, B), BF),
            pltpu.VMEM((2, n_grp, half, B), BF),
            pltpu.VMEM((2, n_grp, half, B), BF),
            pltpu.VMEM((2, zside, half, B), BF),
            pltpu.VMEM((2, zside, half, B), BF),
            pltpu.VMEM((2, 2, half, B), F32),
            dma((2,)),
            dma((4, 2)),
            dma((4, 2)),
            dma((2,)),
            dma((2,)),
            dma((2, n_grp)),
            dma((2, n_grp)),
            dma((2, zside)),
            dma((2, zside)),
            dma((2, zside)),
            dma((2, zside)),
            dma((2,)),
            dma((2,)),
        ],
        compiler_params=pltpu.CompilerParams(
            collective_id=0, has_side_effects=True, vmem_limit_bytes=48 * 1024 * 1024
        ),
    )(features, source_rows, target_codes, block_count, w1, w2, cot)


def solution(mesh):
    n_grp, n_tile = mesh.shape["grp"], mesh.shape["tile"]
    rows = P(("grp", "tile"), None)
    return jax.shard_map(
        functools.partial(on_device, n_grp, n_tile),
        mesh=mesh,
        in_specs=(
            rows,
            P(None, ("grp", "tile"), None),
            P(None, ("grp", "tile")),
            P(("grp", "tile")),
            P(),
            P(),
            rows,
        ),
        out_specs=(rows, rows, P("grp", None), P("grp", None)),
        check_vma=False,
    )
```

```python
import functools
import math

import jax
import jax.numpy as jnp
from jax import lax
from jax.experimental import pallas as pl
from jax.experimental.pallas import tpu as pltpu
from jax.sharding import PartitionSpec as P

MESH = pl.DeviceIdType.MESH
BF = jnp.bfloat16
F32 = jnp.float32
I32 = jnp.int32
UNROLL = 3


def nn(a, b):
    return lax.dot_general(a, b, (((1,), (0,)), ((), ())), preferred_element_type=F32)


def nt(a, b):
    return lax.dot_general(a, b, (((1,), (1,)), ((), ())), preferred_element_type=F32)


def silu_parts(v):
    s = 1.0 / (1.0 + jnp.exp(-v))
    return v * s, s * (1.0 + v * (1.0 - s))


def kernel(
    dims,
    feat_hbm,
    src_hbm,
    codes_hbm,
    count_hbm,
    w_one,
    w_two,
    cot_hbm,
    out_ref,
    dx_ref,
    wg_one,
    wg_two,
    feat,
    src,
    codes,
    count,
    cot,
    ot,
    pt,
    gt,
    wraw,
    wt,
    wc,
    ht,
    hid,
    pre,
    q,
    xs,
    xr,
    qe,
    wgf,
    cs,
    cr,
    sx,
    sf,
    r1,
    r2,
    r3,
    s2,
    r4,
    ab,
    bb,
    fb,
    w_sem,
    i_sem,
    x_send,
    x_recv,
    c_send,
    c_recv,
    g_send,
    g_recv,
    y_send,
    y_recv,
    a_send,
    a_recv,
    b_send,
    b_recv,
    f_send,
    f_recv,
):
    n_grp, n_tile, kvol, rows_k, side, zside = dims
    third = kvol // 3
    B = rows_k
    shard = kvol * B // n_grp
    half = cs.shape[3]
    g = lax.axis_index("grp")
    t = lax.axis_index("tile")
    nz = n_tile // 2
    z = t // 2
    core = t % 2
    gy = g // side
    gx = g % side
    left = lax.rem(t + n_tile - 1, n_tile)
    right = lax.rem(t + 1, n_tile)
    sib = t + 1 - 2 * core
    zlo = z % zside
    zhi = z // zside

    def along(w, first, d):
        y_axis = bool(w) == first
        if y_axis:
            return lax.rem(gy + d, side) * side + gx
        return gy * side + lax.rem(gx + d, side)

    def near_z(d):
        return (zhi * zside + lax.rem(zlo + d, zside)) * 2 + core

    def far_z(d):
        return (lax.rem(zhi + d, zside) * zside + zlo) * 2 + core

    inputs = [
        pltpu.make_async_copy(a, b, i_sem.at[i])
        for i, (a, b) in enumerate(
            (
                (src_hbm, src),
                (codes_hbm, codes),
                (count_hbm, count),
                (feat_hbm, feat),
                (cot_hbm, cot),
            )
        )
    ]
    for c in inputs[:4]:
        c.start()
    for k, w in ((0, w_one), (1, w_two)):
        pltpu.make_async_copy(w, wraw.at[k], w_sem.at[k]).start()
    inputs[4].start()

    barrier = pltpu.get_barrier_semaphore()
    partners = [{"tile": left}, {"tile": right}]
    partners += [{"grp": along(1, True, d)} for d in range(1, side)]
    partners += [{"grp": along(0, True, d)} for d in range(1, side)]
    partners += [{"tile": near_z(d)} for d in range(1, zside)]
    partners += [{"tile": far_z(d)} for d in range(1, zside)]
    for p in partners:
        pl.semaphore_signal(barrier, inc=1, device_id=p, device_id_type=MESH)

    for c in inputs[:4]:
        c.wait()
    two = count[0] - 1
    two_f = two.astype(F32)
    one_f = 1.0 - two_f
    keep_prev = jnp.where(t == 0, 0.0, 1.0)
    keep_next = jnp.where(t == n_tile - 1, 0.0, 1.0)

    for j in range(2):
        ht[:, j * B : (j + 1) * B] = feat[j * B : (j + 1) * B, :].T

    def sweep(body):
        def several(i, carry):
            for n in range(UNROLL):
                body(i * UNROLL + n, carry)
            return carry

        lax.fori_loop(0, third // UNROLL, several, 0)

    iota = lax.broadcasted_iota(I32, (B, B), 0)

    def onehot(k, carry):
        for j in range(2):
            row = src[k, pl.ds(j, 1), :]
            high = codes[j, k] & 1
            live = two if j else 1
            for b in range(2):
                m = (high if b else 1 - high) * live
                idx = row * m + (m - 1)
                hit = jnp.where(iota == idx, 1.0, 0.0).astype(BF)
                ot[k, j * B : (j + 1) * B, b * B : (b + 1) * B] = hit
        return carry

    lax.fori_loop(0, kvol, onehot, 0)

    def prep(w):
        pltpu.make_async_copy(w_two if w else w_one, wraw.at[w], w_sem.at[w]).wait()

        def body(i, carry):
            for pos, cls in enumerate((1, 0, 2)):
                at = pl.multiple_of((pos * third + i) * B, B)
                block = wraw[w, 3 * i + cls]
                wc[w, :, pl.ds(at, B)] = block
                wt[w, :, pl.ds(at, B)] = block.T
            return carry

        sweep(body)

    n1 = third * B

    def put(slot, i, value):
        at = pl.multiple_of((slot * third + i) * B, B)
        pt[pl.ds(at, B), :] = value.astype(BF)

    def forward_edges(field, w):
        def body(i, carry):
            put(2, i, nn(field[:, :B], ot[3 * i, :B, :]))
            put(3, i, nn(field[:, :B], ot[3 * i + 2, :B, :]))
            put(4, i, nn(field[:, B:], ot[3 * i + 2, B:, :]))
            return carry

        sweep(body)
        to_prev = nn(wt[w, :, n1 : 2 * n1], pt[2 * n1 : 3 * n1, :])
        part_a = nn(wt[w, :, 2 * n1 :], pt[3 * n1 : 4 * n1, :])
        part_b = nn(wt[w, :, 2 * n1 :], pt[4 * n1 :, :])
        xs[w, 0] = to_prev.astype(BF)
        xs[w, 1] = (part_b + part_a * one_f).astype(BF)
        return part_a * two_f

    def forward_own(field, w):
        def body(i, carry):
            put(0, i, nn(field[...], ot[3 * i + 1]))
            put(1, i, nn(field[:, B:], ot[3 * i, B:, :]))
            return carry

        sweep(body)
        return nn(wt[w, :, : 2 * n1], pt[: 2 * n1, :])

    def exchange(e, to_prev, to_next):
        return [
            pltpu.make_async_remote_copy(
                src_ref=to_prev,
                dst_ref=xr.at[e, 1],
                send_sem=x_send.at[e, 1],
                recv_sem=x_recv.at[e, 1],
                device_id={"tile": left},
                device_id_type=MESH,
            ),
            pltpu.make_async_remote_copy(
                src_ref=to_next,
                dst_ref=xr.at[e, 0],
                send_sem=x_send.at[e, 0],
                recv_sem=x_recv.at[e, 0],
                device_id={"tile": right},
                device_id_type=MESH,
            ),
        ]

    def from_sides(e):
        return (
            xr[e, 0].astype(F32) * keep_prev,
            xr[e, 1].astype(F32) * keep_next,
        )

    def start(copies):
        for c in copies:
            c.start()
        return copies

    def landed(copies):
        for c in copies:
            c.wait_recv()

    pending = []
    mask = jnp.where(
        lax.broadcasted_iota(I32, (1, 2 * B), 1) < B * count[0], 1.0, 0.0
    )

    prep(0)
    extra = forward_edges(ht, 0)
    pl.semaphore_wait(barrier, len(partners))
    moved = start(exchange(0, xs.at[0, 0], xs.at[0, 1]))
    pending += moved
    own = forward_own(ht, 0) + extra
    prep(1)
    landed(moved)
    before, after = from_sides(0)
    pre_one = own + before + after
    pre[...] = pre_one
    hid[...] = (silu_parts(pre_one)[0] * mask).astype(BF)

    extra = forward_edges(hid, 1)
    moved = start(exchange(1, xs.at[1, 0], xs.at[1, 1]))
    pending += moved
    own = forward_own(hid, 1) + extra + ht[...].astype(F32)
    inputs[4].wait()
    cot_t = jnp.concatenate(
        [cot[:B, :].astype(F32).T, cot[B:, :].astype(F32).T], axis=1
    )
    landed(moved)
    before, after = from_sides(1)
    total = own + before + after
    value, slope = silu_parts(total)
    q[1] = (cot_t * slope * mask).astype(BF)
    moved = start(exchange(2, q.at[1], q.at[1]))
    pending += moved
    result = value * mask
    for j in range(2):
        out_ref[j * B : (j + 1) * B, :] = result[:, j * B : (j + 1) * B].T.astype(BF)

    def put_g(pos, i, lo, hi, v):
        at = pl.multiple_of((pos * third + i) * B, B)
        gt[pl.ds(at, B), lo:hi] = v.astype(BF)

    def back_own(w):
        def body(i, carry):
            put_g(0, i, 0, 2 * B, nt(q[w], ot[3 * i + 1]))
            put_g(1, i, B, 2 * B, nt(q[w], ot[3 * i, B:, :]))
            return carry

        sweep(body)

    def back_edges(w, e):
        before, after = from_sides(e)
        mixed = (after * one_f + q[w].astype(F32) * two_f).astype(BF)
        before = before.astype(BF)
        after = after.astype(BF)
        qe[0] = before
        qe[1] = mixed
        qe[2] = after

        def body(i, carry):
            put_g(1, i, 0, B, nt(qe[0], ot[3 * i, :B, :]))
            put_g(2, i, 0, B, nt(qe[1], ot[3 * i + 2, :B, :]))
            put_g(2, i, B, 2 * B, nt(qe[2], ot[3 * i + 2, B:, :]))
            return carry

        sweep(body)

    def weight_grads(field, w):
        def body(i, carry):
            for pos, cls in enumerate((1, 0, 2)):
                at = pl.multiple_of((pos * third + i) * B, B)
                to = pl.multiple_of((3 * i + cls) * B, B)
                wgf[w, pl.ds(to, B), :] = nt(field[...], gt[pl.ds(at, B), :])
            return carry

        sweep(body)

    def half_rows(w, rel, b, h):
        a = lax.rem((gy if w else gx) + rel, side)
        s = a * side + b if w else b * side + a
        at = pl.multiple_of(s * shard + h * half, 8)
        return wgf[w, pl.ds(at, half), :]

    order = (2, 1, 3, 0)
    spans = ((0, 1), (1, 3), (3, 4))

    def send_pair(w):
        copies = []
        for n, (lo, hi) in enumerate(spans):
            for p in range(lo, hi):

                def body(b, carry, p=p):
                    cs[w, p, b] = half_rows(w, order[p], b, 1 - core).astype(BF)
                    return carry

                lax.fori_loop(0, side, body, 0)
            copies += start(
                [
                    pltpu.make_async_remote_copy(
                        src_ref=cs.at[w, pl.ds(lo, hi - lo)],
                        dst_ref=cr.at[w, pl.ds(lo, hi - lo)],
                        send_sem=c_send.at[w, n],
                        recv_sem=c_recv.at[w, n],
                        device_id={"tile": sib},
                        device_id_type=MESH,
                    )
                ]
            )
        return copies

    def pair_sum(w, p):
        def body(b, carry):
            mine = half_rows(w, order[p], b, core)
            sx[w, p, b] = (mine + cr[w, p, b].astype(F32)).astype(BF)
            return carry

        lax.fori_loop(0, side, body, 0)

    mid = side // 2

    def ring_copy(w, n, src_ref, dst_ref, d):
        return pltpu.make_async_remote_copy(
            src_ref=src_ref,
            dst_ref=dst_ref,
            send_sem=g_send.at[w, n],
            recv_sem=g_recv.at[w, n],
            device_id={"grp": along(w, True, d)},
            device_id_type=MESH,
        )

    def ring_open(w, pair):
        landed(pair[:1])
        pair_sum(w, 0)
        lo, hi = pl.ds(0, mid), pl.ds(mid, mid)
        first = start(
            [
                ring_copy(w, 0, sx.at[w, 0, lo], r1.at[w, 0], 1),
                ring_copy(w, 1, sx.at[w, 0, hi], r1.at[w, 1], side - 1),
            ]
        )
        landed(pair[1:2])
        pair_sum(w, 1)
        pair_sum(w, 2)
        second = start(
            [
                ring_copy(w, 2, sx.at[w, 1, hi], r2.at[w, 0], 1),
                ring_copy(w, 3, sx.at[w, 2, lo], r2.at[w, 1], side - 1),
            ]
        )
        return first, second

    def ring_close(w, first):
        landed(first)
        third_leg = []
        for n, (p, base, d) in enumerate(((1, 0, 1), (2, mid, side - 1))):

            def body(b, carry, n=n, p=p, base=base):
                v = sx[w, p, base + b].astype(F32) + r1[w, n, b].astype(F32)
                sf[w, n, b] = v.astype(BF)
                return carry

            lax.fori_loop(0, mid, body, 0)
            third_leg += start([ring_copy(w, 4 + n, sf.at[w, n], r3.at[w, n], d)])
        return third_leg

    def cross(w, pair, second, third_leg):
        landed(pair[2:])
        pair_sum(w, 3)
        landed(second)
        landed(third_leg)
        for n in range(2):

            def body(b, carry, n=n):
                v = sx[w, 3, n * mid + b].astype(F32)
                v = v + r3[w, n, b].astype(F32) + r2[w, 1 - n, b].astype(F32)
                s2[w, n * mid + b] = v.astype(BF)
                return carry

            lax.fori_loop(0, mid, body, 0)
        here = gx if w else gy
        return start(
            [
                pltpu.make_async_remote_copy(
                    src_ref=s2.at[w, lax.rem(here + d, side)],
                    dst_ref=r4.at[w, d],
                    send_sem=y_send.at[w, d],
                    recv_sem=y_recv.at[w, d],
                    device_id={"grp": along(w, False, d)},
                    device_id_type=MESH,
                )
                for d in range(1, side)
            ]
        )

    def send_near(w, moved):
        landed(moved)
        acc = s2[w, gx if w else gy].astype(F32)
        for d in range(1, side):
            acc = acc + r4[w, d].astype(F32)
        ab[w, zlo] = acc.astype(BF)
        return start(
            [
                pltpu.make_async_remote_copy(
                    src_ref=ab.at[w, zlo],
                    dst_ref=ab.at[w, zlo],
                    send_sem=a_send.at[w, d],
                    recv_sem=a_recv.at[w, d],
                    device_id={"tile": near_z(d)},
                    device_id_type=MESH,
                )
                for d in range(1, zside)
            ]
        )

    def send_far(w, moved):
        landed(moved)
        acc = ab[w, 0].astype(F32)
        for d in range(1, zside):
            acc = acc + ab[w, d].astype(F32)
        bb[w, zhi] = acc.astype(BF)
        return start(
            [
                pltpu.make_async_remote_copy(
                    src_ref=bb.at[w, zhi],
                    dst_ref=bb.at[w, zhi],
                    send_sem=b_send.at[w, d],
                    recv_sem=b_recv.at[w, d],
                    device_id={"tile": far_z(d)},
                    device_id_type=MESH,
                )
                for d in range(1, zside)
            ]
        )

    def send_last(w, moved):
        landed(moved)
        acc = bb[w, 0].astype(F32)
        for d in range(1, zside):
            acc = acc + bb[w, d].astype(F32)
        fb[w, core] = acc
        return start(
            [
                pltpu.make_async_remote_copy(
                    src_ref=fb.at[w, core],
                    dst_ref=fb.at[w, core],
                    send_sem=f_send.at[w],
                    recv_sem=f_recv.at[w],
                    device_id={"tile": sib},
                    device_id_type=MESH,
                )
            ]
        )

    scale = float(n_grp * n_tile * 2 * B) ** (-0.5)

    def finish(w, moved):
        landed(moved)
        dst = wg_two if w else wg_one
        dst[:half, :] = fb[w, 0] * scale
        dst[half:, :] = fb[w, 1, : shard - half, :] * scale

    for w in range(2 if wgf.shape[1] > kvol * B else 0):
        wgf[w, kvol * B :, :] = jnp.zeros((wgf.shape[1] - kvol * B, B), F32)

    back_own(1)
    landed(moved)
    back_edges(1, 2)
    grad_mid = nn(wc[1], gt[...])
    slope = silu_parts(pre[...])[1]
    q[0] = (grad_mid * slope * mask).astype(BF)
    moved = start(exchange(3, q.at[0], q.at[0]))
    pending += moved
    weight_grads(hid, 1)
    pair_two = send_pair(1)
    back_own(0)
    first_two, second_two = ring_open(1, pair_two)
    landed(moved)
    back_edges(0, 3)
    weight_grads(ht, 0)
    pair_one = send_pair(0)
    third_two = ring_close(1, first_two)
    first_one, second_one = ring_open(0, pair_one)
    cross_two = cross(1, pair_two, second_two, third_two)
    third_one = ring_close(0, first_one)
    grad_in = nn(wc[0], gt[...]) + q[1].astype(F32)
    cross_one = cross(0, pair_one, second_one, third_one)
    near_two = send_near(1, cross_two)
    for j in range(2):
        dx_ref[j * B : (j + 1) * B, :] = grad_in[:, j * B : (j + 1) * B].T.astype(BF)
    near_one = send_near(0, cross_one)
    far_two = send_far(1, near_two)
    far_one = send_far(0, near_one)
    last_two = send_last(1, far_two)
    finish(1, last_two)
    last_one = send_last(0, far_one)
    finish(0, last_one)
    for w in (pair_two, first_two, second_two, third_two, cross_two, near_two):
        pending += w
    for w in (pair_one, first_one, second_one, third_one, cross_one, near_one):
        pending += w
    pending += far_two + far_one + last_two + last_one
    for c in pending:
        c.wait_send()


def settle(*refs):
    sem = refs[8]
    copies = [pltpu.make_async_copy(refs[i], refs[4 + i], sem.at[i]) for i in range(4)]
    for c in copies:
        c.start()
    for c in copies:
        c.wait()


def on_device(n_grp, n_tile, features, source_rows, target_codes, block_count, w1, w2, cot):
    kvol, _, B = source_rows.shape
    side = math.isqrt(n_grp)
    zside = math.isqrt(n_tile // 2)
    shard = kvol * B // n_grp
    half = -(-shard // 32) * 16
    wide = kvol * B
    vmem = pl.BlockSpec(memory_space=pltpu.VMEM)
    hbm = pl.BlockSpec(memory_space=pltpu.HBM)
    dma = pltpu.SemaphoreType.DMA
    dims = (n_grp, n_tile, kvol, B, side, zside)
    results = pl.pallas_call(
        functools.partial(kernel, dims),
        out_shape=(
            jax.ShapeDtypeStruct((2 * B, B), BF),
            jax.ShapeDtypeStruct((2 * B, B), BF),
            jax.ShapeDtypeStruct((shard, B), F32),
            jax.ShapeDtypeStruct((shard, B), F32),
        ),
        in_specs=[hbm] * 7,
        out_specs=(vmem,) * 4,
        scratch_shapes=[
            pltpu.VMEM((2 * B, B), BF),
            pltpu.VMEM((kvol, 2, B), I32),
            pltpu.SMEM((2, kvol), I32),
            pltpu.SMEM((1,), I32),
            pltpu.VMEM((2 * B, B), BF),
            pltpu.VMEM((kvol, 2 * B, 2 * B), BF),
            pltpu.VMEM((5 * (kvol // 3) * B, 2 * B), BF),
            pltpu.VMEM((wide, 2 * B), BF),
            pltpu.VMEM((2, kvol, B, B), BF),
            pltpu.VMEM((2, B, wide), BF),
            pltpu.VMEM((2, B, wide), BF),
            pltpu.VMEM((B, 2 * B), BF),
            pltpu.VMEM((B, 2 * B), BF),
            pltpu.VMEM((B, 2 * B), F32),
            pltpu.VMEM((2, B, 2 * B), BF),
            pltpu.VMEM((2, 2, B, 2 * B), BF),
            pltpu.VMEM((4, 2, B, 2 * B), BF),
            pltpu.VMEM((3, B, 2 * B), BF),
            pltpu.VMEM((2, wide + 2 * half - shard, B), F32),
            pltpu.VMEM((2, side, side, half, B), BF),
            pltpu.VMEM((2, side, side, half, B), BF),
            pltpu.VMEM((2, side, side, half, B), BF),
            pltpu.VMEM((2, 2, side // 2, half, B), BF),
            pltpu.VMEM((2, 2, side // 2, half, B), BF),
            pltpu.VMEM((2, 2, side // 2, half, B), BF),
            pltpu.VMEM((2, 2, side // 2, half, B), BF),
            pltpu.VMEM((2, side, half, B), BF),
            pltpu.VMEM((2, side, half, B), BF),
            pltpu.VMEM((2, zside, half, B), BF),
            pltpu.VMEM((2, zside, half, B), BF),
            pltpu.VMEM((2, 2, half, B), F32),
            dma((2,)),
            dma((5,)),
            dma((4, 2)),
            dma((4, 2)),
            dma((2, 3)),
            dma((2, 3)),
            dma((2, 6)),
            dma((2, 6)),
            dma((2, side)),
            dma((2, side)),
            dma((2, zside)),
            dma((2, zside)),
            dma((2, zside)),
            dma((2, zside)),
            dma((2,)),
            dma((2,)),
        ],
        compiler_params=pltpu.CompilerParams(
            collective_id=0, has_side_effects=True, vmem_limit_bytes=67043328
        ),
    )(features, source_rows, target_codes.T, block_count, w1, w2, cot)
    return pl.pallas_call(
        settle,
        out_shape=tuple(jax.ShapeDtypeStruct(r.shape, r.dtype) for r in results),
        in_specs=[vmem] * 4,
        out_specs=(hbm,) * 4,
        scratch_shapes=[dma((4,))],
    )(*results)


def solution(mesh):
    n_grp, n_tile = mesh.shape["grp"], mesh.shape["tile"]
    rows = P(("grp", "tile"), None)
    return jax.shard_map(
        functools.partial(on_device, n_grp, n_tile),
        mesh=mesh,
        in_specs=(
            rows,
            P(None, ("grp", "tile"), None),
            P(None, ("grp", "tile")),
            P(("grp", "tile")),
            P(),
            P(),
            rows,
        ),
        out_specs=(rows, rows, P("grp", None), P("grp", None)),
        check_vma=False,
    )
```

```python
import functools
import math

import jax
import jax.numpy as jnp
from jax import lax
from jax.experimental import pallas as pl
from jax.experimental.pallas import tpu as pltpu
from jax.sharding import PartitionSpec as P

MESH = pl.DeviceIdType.MESH
BF = jnp.bfloat16
F32 = jnp.float32
I32 = jnp.int32
UNROLL = 9


def nn(a, b):
    return lax.dot_general(a, b, (((1,), (0,)), ((), ())), preferred_element_type=F32)


def nt(a, b):
    return lax.dot_general(a, b, (((1,), (1,)), ((), ())), preferred_element_type=F32)


def silu_parts(v):
    s = 1.0 / (1.0 + jnp.exp(-v))
    return v * s, s * (1.0 + v * (1.0 - s))


def kernel(
    dims,
    feat_hbm,
    src_hbm,
    codes_hbm,
    count_hbm,
    w_one,
    w_two,
    cot_hbm,
    out_ref,
    dx_ref,
    wg_one,
    wg_two,
    feat,
    src,
    codes,
    count,
    cot,
    ot,
    pt,
    gt,
    wraw,
    wt,
    wc,
    ht,
    hid,
    pre,
    q,
    xs,
    xr,
    qe,
    hl,
    wgf,
    cs,
    cr,
    sx,
    sf,
    r1,
    r2,
    r3,
    s2,
    r4,
    ab,
    bb,
    fb,
    w_sem,
    i_sem,
    x_send,
    x_recv,
    c_send,
    c_recv,
    g_send,
    g_recv,
    y_send,
    y_recv,
    a_send,
    a_recv,
    b_send,
    b_recv,
    f_send,
    f_recv,
):
    n_grp, n_tile, kvol, rows_k, side, zside = dims
    third = kvol // 3
    B = rows_k
    shard = kvol * B // n_grp
    half = cs.shape[3]
    g = lax.axis_index("grp")
    t = lax.axis_index("tile")
    nz = n_tile // 2
    z = t // 2
    core = t % 2
    gy = g // side
    gx = g % side
    left = lax.rem(t + n_tile - 1, n_tile)
    right = lax.rem(t + 1, n_tile)
    sib = t + 1 - 2 * core
    zlo = z % zside
    zhi = z // zside

    def along(axis, d):
        if axis:
            return gy * side + lax.rem(gx + d, side)
        return lax.rem(gy + d, side) * side + gx

    def near_z(d):
        return (zhi * zside + lax.rem(zlo + d, zside)) * 2 + core

    def far_z(d):
        return (lax.rem(zhi + d, zside) * zside + zlo) * 2 + core

    inputs = [
        pltpu.make_async_copy(a, b, i_sem.at[i])
        for i, (a, b) in enumerate(
            (
                (src_hbm, src),
                (codes_hbm, codes),
                (count_hbm, count),
                (feat_hbm, feat),
                (cot_hbm, cot),
            )
        )
    ]
    for c in inputs[:4]:
        c.start()
    for k, w in ((0, w_one), (1, w_two)):
        pltpu.make_async_copy(w, wraw.at[k], w_sem.at[k]).start()
    inputs[4].start()

    barrier = pltpu.get_barrier_semaphore()
    partners = [{"tile": left}, {"tile": right}]
    partners += [{"grp": along(axis, d)} for axis in range(2) for d in range(1, side)]
    partners += [{"tile": near_z(d)} for d in range(1, zside)]
    partners += [{"tile": far_z(d)} for d in range(1, zside)]
    for p in partners:
        pl.semaphore_signal(barrier, inc=1, device_id=p, device_id_type=MESH)

    for c in inputs[:4]:
        c.wait()
    two = count[0] - 1
    two_f = two.astype(F32)
    one_f = 1.0 - two_f
    keep_prev = jnp.where(t == 0, 0.0, 1.0)
    keep_next = jnp.where(t == n_tile - 1, 0.0, 1.0)

    for j in range(2):
        ht[:, j * B : (j + 1) * B] = feat[j * B : (j + 1) * B, :].T

    def sweep(body):
        def several(i, carry):
            for n in range(UNROLL):
                body(i * UNROLL + n, carry)
            return carry

        lax.fori_loop(0, third // UNROLL, several, 0)

    iota = lax.broadcasted_iota(I32, (B, B), 0)

    def fill(k, at, row, high, live):
        for b in range(2):
            m = (high if b else 1 - high) * live
            idx = row * m + (m - 1)
            hit = jnp.where(iota == idx, 1.0, 0.0).astype(BF)
            ot[k, at : at + B, b * B : (b + 1) * B] = hit

    def entry(k, j):
        return src[k, pl.ds(j, 1), :], codes[j, k] & 1

    def fill_edges(i, carry):
        row, high = entry(3 * i, 0)
        fill(3 * i, 0, row, high, 1)
        k = 3 * i + 2
        row, high = entry(k, 0)
        row_b, high_b = entry(k, 1)
        row = row * (1 - two) + row_b * two
        high = high * (1 - two) + high_b * two
        fill(k, B, row, high, 1)

    def fill_own(i, carry):
        k = 3 * i + 1
        for j in range(2):
            row, high = entry(k, j)
            fill(k, j * B, row, high, two if j else 1)
        row, high = entry(3 * i, 1)
        fill(3 * i, B, row, high, two)
        row, high = entry(3 * i + 2, 0)
        fill(3 * i + 2, 0, row, high, two)

    sweep(fill_edges)

    slots = {1: 0, 0: 1, 2: 2}

    def prep_t(w, classes):
        def body(i, carry):
            for cls in classes:
                at = pl.multiple_of((slots[cls] * third + i) * B, B)
                wt[w, :, pl.ds(at, B)] = wraw[w, 3 * i + cls].T

        sweep(body)

    def prep_c(w):
        def body(i, carry):
            for cls in range(3):
                at = pl.multiple_of((slots[cls] * third + i) * B, B)
                wc[w, :, pl.ds(at, B)] = wraw[w, 3 * i + cls]

        sweep(body)

    def weights_here(w):
        pltpu.make_async_copy(w_two if w else w_one, wraw.at[w], w_sem.at[w]).wait()

    n1 = third * B

    def put(slot, i, value):
        at = pl.multiple_of((slot * third + i) * B, B)
        pt[pl.ds(at, B), :] = value.astype(BF)

    def forward_edges(field, w):
        v = field[:, :B].astype(F32) * one_f + field[:, B:].astype(F32) * two_f
        hl[...] = v.astype(BF)

        def body(i, carry):
            put(3, i, nn(field[:, :B], ot[3 * i, :B, :]))
            put(4, i, nn(hl[...], ot[3 * i + 2, B:, :]))

        sweep(body)
        to_prev = nn(wt[w, :, n1 : 2 * n1], pt[3 * n1 : 4 * n1, :])
        to_next = nn(wt[w, :, 2 * n1 :], pt[4 * n1 :, :])
        xs[w, 0] = to_prev.astype(BF)
        xs[w, 1] = to_next.astype(BF)

    def forward_own(field, w):
        def body(i, carry):
            put(0, i, nn(field[...], ot[3 * i + 1]))
            put(1, i, nn(field[:, B:], ot[3 * i, B:, :]))
            put(2, i, nn(field[:, :B], ot[3 * i + 2, :B, :]))

        sweep(body)
        return nn(wt[w], pt[: 3 * n1, :])

    def exchange(e, to_prev, to_next):
        return [
            pltpu.make_async_remote_copy(
                src_ref=to_prev,
                dst_ref=xr.at[e, 1],
                send_sem=x_send.at[e, 1],
                recv_sem=x_recv.at[e, 1],
                device_id={"tile": left},
                device_id_type=MESH,
            ),
            pltpu.make_async_remote_copy(
                src_ref=to_next,
                dst_ref=xr.at[e, 0],
                send_sem=x_send.at[e, 0],
                recv_sem=x_recv.at[e, 0],
                device_id={"tile": right},
                device_id_type=MESH,
            ),
        ]

    def from_sides(e):
        return (
            xr[e, 0].astype(F32) * keep_prev,
            xr[e, 1].astype(F32) * keep_next,
        )

    def start(copies):
        for c in copies:
            c.start()
        return copies

    def landed(copies):
        for c in copies:
            c.wait_recv()

    pending = []
    mask = jnp.where(
        lax.broadcasted_iota(I32, (1, 2 * B), 1) < B * count[0], 1.0, 0.0
    )

    weights_here(0)
    prep_t(0, (0, 2))
    forward_edges(ht, 0)
    pl.semaphore_wait(barrier, len(partners))
    moved = start(exchange(0, xs.at[0, 0], xs.at[0, 1]))
    pending += moved
    sweep(fill_own)
    prep_t(0, (1,))
    own = forward_own(ht, 0)
    weights_here(1)
    prep_t(1, (0, 1, 2))
    landed(moved)
    before, after = from_sides(0)
    pre_one = own + before + after
    pre[...] = pre_one
    hid[...] = (silu_parts(pre_one)[0] * mask).astype(BF)

    forward_edges(hid, 1)
    moved = start(exchange(1, xs.at[1, 0], xs.at[1, 1]))
    pending += moved
    own = forward_own(hid, 1) + ht[...].astype(F32)
    prep_c(1)
    inputs[4].wait()
    cot_t = jnp.concatenate(
        [cot[:B, :].astype(F32).T, cot[B:, :].astype(F32).T], axis=1
    )
    landed(moved)
    before, after = from_sides(1)
    total = own + before + after
    value, slope = silu_parts(total)
    q[1] = (cot_t * slope * mask).astype(BF)
    moved = start(exchange(2, q.at[1], q.at[1]))
    pending += moved
    result = value * mask
    for j in range(2):
        out_ref[j * B : (j + 1) * B, :] = result[:, j * B : (j + 1) * B].T.astype(BF)

    def put_g(pos, i, lo, hi, v):
        at = pl.multiple_of((pos * third + i) * B, B)
        gt[pl.ds(at, B), lo:hi] = v.astype(BF)

    def back_own(w):
        def body(i, carry):
            put_g(0, i, 0, 2 * B, nt(q[w], ot[3 * i + 1]))
            put_g(1, i, B, 2 * B, nt(q[w], ot[3 * i, B:, :]))
            put_g(2, i, 0, B, nt(q[w], ot[3 * i + 2, :B, :]))

        sweep(body)

    def back_edges(w, e):
        before, after = from_sides(e)
        qe[0] = before.astype(BF)
        qe[1] = after.astype(BF)

        def body(i, carry):
            put_g(1, i, 0, B, nt(qe[0], ot[3 * i, :B, :]))
            last = nt(qe[1], ot[3 * i + 2, B:, :])
            at = pl.multiple_of((2 * third + i) * B, B)
            lower = gt[pl.ds(at, B), :B].astype(F32)
            put_g(2, i, 0, B, lower + last * one_f)
            put_g(2, i, B, 2 * B, last * two_f)

        sweep(body)

    def weight_grads(field, w, classes):
        def body(i, carry):
            for cls in classes:
                at = pl.multiple_of((slots[cls] * third + i) * B, B)
                to = pl.multiple_of((3 * i + cls) * B, B)
                wgf[w, pl.ds(to, B), :] = nt(field[...], gt[pl.ds(at, B), :])

        sweep(body)

    cut = -(-half // 32) * 16
    rows = (pl.ds(0, cut), pl.ds(cut, half - cut))

    def half_rows(w, r, rel, b, h):
        a = lax.rem((gx if r else gy) + rel, side)
        s = b * side + a if r else a * side + b
        at = pl.multiple_of(s * shard + h * half + rows[r].start, 8)
        return wgf[w, pl.ds(at, rows[r].size), :]

    order = (2, 1, 3, 0)
    spans = ((0, 1), (1, 3), (3, 4))

    def send_pair(w):
        copies = []
        for n, (lo, hi) in enumerate(spans):
            for p in range(lo, hi):

                def body(b, carry, p=p):
                    for r in range(2):
                        v = half_rows(w, r, order[p], b, 1 - core)
                        cs[w, p, b, rows[r]] = v.astype(BF)
                    return carry

                lax.fori_loop(0, side, body, 0)
            copies += start(
                [
                    pltpu.make_async_remote_copy(
                        src_ref=cs.at[w, pl.ds(lo, hi - lo)],
                        dst_ref=cr.at[w, pl.ds(lo, hi - lo)],
                        send_sem=c_send.at[w, n],
                        recv_sem=c_recv.at[w, n],
                        device_id={"tile": sib},
                        device_id_type=MESH,
                    )
                ]
            )
        return copies

    def pair_sum(w, p):
        def body(b, carry):
            for r in range(2):
                v = half_rows(w, r, order[p], b, core)
                v = v + cr[w, p, b, rows[r]].astype(F32)
                sx[w, p, b, rows[r]] = v.astype(BF)
            return carry

        lax.fori_loop(0, side, body, 0)

    mid = side // 2
    low, top = pl.ds(0, mid), pl.ds(mid, mid)

    def ring_copy(w, r, n, src_ref, dst_ref, d):
        return pltpu.make_async_remote_copy(
            src_ref=src_ref.at[:, rows[r]],
            dst_ref=dst_ref.at[:, rows[r]],
            send_sem=g_send.at[w, r, n],
            recv_sem=g_recv.at[w, r, n],
            device_id={"grp": along(r, d)},
            device_id_type=MESH,
        )

    def ring_open(w, pair):
        landed(pair[:1])
        pair_sum(w, 0)
        first, second = [], []
        for r in range(2):
            first += start(
                [
                    ring_copy(w, r, 0, sx.at[w, 0, low], r1.at[w, 0], 1),
                    ring_copy(w, r, 1, sx.at[w, 0, top], r1.at[w, 1], side - 1),
                ]
            )
        landed(pair[1:2])
        pair_sum(w, 1)
        pair_sum(w, 2)
        for r in range(2):
            second += start(
                [
                    ring_copy(w, r, 2, sx.at[w, 1, top], r2.at[w, 0], 1),
                    ring_copy(w, r, 3, sx.at[w, 2, low], r2.at[w, 1], side - 1),
                ]
            )
        return first, second

    def ring_close(w, first):
        landed(first)
        third_leg = []
        for n, (p, base, d) in enumerate(((1, 0, 1), (2, mid, side - 1))):

            def body(b, carry, n=n, p=p, base=base):
                v = sx[w, p, base + b].astype(F32) + r1[w, n, b].astype(F32)
                sf[w, n, b] = v.astype(BF)
                return carry

            lax.fori_loop(0, mid, body, 0)
            for r in range(2):
                third_leg += start(
                    [ring_copy(w, r, 4 + n, sf.at[w, n], r3.at[w, n], d)]
                )
        return third_leg

    def cross(w, pair, second, third_leg):
        landed(pair[2:])
        pair_sum(w, 3)
        landed(second)
        landed(third_leg)
        for n in range(2):

            def body(b, carry, n=n):
                v = sx[w, 3, n * mid + b].astype(F32)
                v = v + r3[w, n, b].astype(F32) + r2[w, 1 - n, b].astype(F32)
                s2[w, n * mid + b] = v.astype(BF)
                return carry

            lax.fori_loop(0, mid, body, 0)
        return start(
            [
                pltpu.make_async_remote_copy(
                    src_ref=s2.at[w, lax.rem((gy if r else gx) + d, side), rows[r]],
                    dst_ref=r4.at[w, d, rows[r]],
                    send_sem=y_send.at[w, r, d],
                    recv_sem=y_recv.at[w, r, d],
                    device_id={"grp": along(1 - r, d)},
                    device_id_type=MESH,
                )
                for d in (2, 1, 3)
                for r in range(2)
            ]
        )

    def send_near(w, moved):
        landed(moved)
        for r in range(2):
            acc = s2[w, gy if r else gx, rows[r]].astype(F32)
            for d in range(1, side):
                acc = acc + r4[w, d, rows[r]].astype(F32)
            ab[w, zlo, rows[r]] = acc.astype(BF)
        return start(
            [
                pltpu.make_async_remote_copy(
                    src_ref=ab.at[w, zlo],
                    dst_ref=ab.at[w, zlo],
                    send_sem=a_send.at[w, d],
                    recv_sem=a_recv.at[w, d],
                    device_id={"tile": near_z(d)},
                    device_id_type=MESH,
                )
                for d in range(1, zside)
            ]
        )

    def send_far(w, moved):
        landed(moved)
        acc = ab[w, 0].astype(F32)
        for d in range(1, zside):
            acc = acc + ab[w, d].astype(F32)
        bb[w, zhi] = acc.astype(BF)
        return start(
            [
                pltpu.make_async_remote_copy(
                    src_ref=bb.at[w, zhi],
                    dst_ref=bb.at[w, zhi],
                    send_sem=b_send.at[w, d],
                    recv_sem=b_recv.at[w, d],
                    device_id={"tile": far_z(d)},
                    device_id_type=MESH,
                )
                for d in range(1, zside)
            ]
        )

    def send_last(w, moved):
        landed(moved)
        acc = bb[w, 0].astype(F32)
        for d in range(1, zside):
            acc = acc + bb[w, d].astype(F32)
        fb[w, core] = acc
        return start(
            [
                pltpu.make_async_remote_copy(
                    src_ref=fb.at[w, core],
                    dst_ref=fb.at[w, core],
                    send_sem=f_send.at[w],
                    recv_sem=f_recv.at[w],
                    device_id={"tile": sib},
                    device_id_type=MESH,
                )
            ]
        )

    scale = float(n_grp * n_tile * 2 * B) ** (-0.5)

    def finish(w, moved):
        landed(moved)
        dst = wg_two if w else wg_one
        dst[:half, :] = fb[w, 0] * scale
        dst[half:, :] = fb[w, 1, : shard - half, :] * scale

    for w in range(2 if wgf.shape[1] > kvol * B else 0):
        wgf[w, kvol * B :, :] = jnp.zeros((wgf.shape[1] - kvol * B, B), F32)

    back_own(1)
    landed(moved)
    back_edges(1, 2)
    grad_mid = nn(wc[1], gt[...])
    slope = silu_parts(pre[...])[1]
    q[0] = (grad_mid * slope * mask).astype(BF)
    moved = start(exchange(3, q.at[0], q.at[0]))
    pending += moved
    weight_grads(hid, 1, (0, 1, 2))
    pair_two = send_pair(1)
    back_own(0)
    weight_grads(ht, 0, (1,))
    first_two, second_two = ring_open(1, pair_two)
    landed(moved)
    back_edges(0, 3)
    weight_grads(ht, 0, (0, 2))
    pair_one = send_pair(0)
    third_two = ring_close(1, first_two)
    first_one, second_one = ring_open(0, pair_one)
    cross_two = cross(1, pair_two, second_two, third_two)
    third_one = ring_close(0, first_one)
    prep_c(0)
    grad_in = nn(wc[0], gt[...]) + q[1].astype(F32)
    cross_one = cross(0, pair_one, second_one, third_one)
    near_two = send_near(1, cross_two)
    for j in range(2):
        dx_ref[j * B : (j + 1) * B, :] = grad_in[:, j * B : (j + 1) * B].T.astype(BF)
    near_one = send_near(0, cross_one)
    far_two = send_far(1, near_two)
    far_one = send_far(0, near_one)
    last_two = send_last(1, far_two)
    finish(1, last_two)
    last_one = send_last(0, far_one)
    finish(0, last_one)
    for w in (pair_two, first_two, second_two, third_two, cross_two, near_two):
        pending += w
    for w in (pair_one, first_one, second_one, third_one, cross_one, near_one):
        pending += w
    pending += far_two + far_one + last_two + last_one
    for c in pending:
        c.wait_send()


def settle(*refs):
    sem = refs[8]
    copies = [pltpu.make_async_copy(refs[i], refs[4 + i], sem.at[i]) for i in range(4)]
    for c in copies:
        c.start()
    for c in copies:
        c.wait()


def on_device(n_grp, n_tile, features, source_rows, target_codes, block_count, w1, w2, cot):
    kvol, _, B = source_rows.shape
    side = math.isqrt(n_grp)
    zside = math.isqrt(n_tile // 2)
    shard = kvol * B // n_grp
    half = -(-shard // 32) * 16
    wide = kvol * B
    vmem = pl.BlockSpec(memory_space=pltpu.VMEM)
    hbm = pl.BlockSpec(memory_space=pltpu.HBM)
    dma = pltpu.SemaphoreType.DMA
    dims = (n_grp, n_tile, kvol, B, side, zside)
    results = pl.pallas_call(
        functools.partial(kernel, dims),
        out_shape=(
            jax.ShapeDtypeStruct((2 * B, B), BF),
            jax.ShapeDtypeStruct((2 * B, B), BF),
            jax.ShapeDtypeStruct((shard, B), F32),
            jax.ShapeDtypeStruct((shard, B), F32),
        ),
        in_specs=[hbm] * 7,
        out_specs=(vmem,) * 4,
        scratch_shapes=[
            pltpu.VMEM((2 * B, B), BF),
            pltpu.VMEM((kvol, 2, B), I32),
            pltpu.SMEM((2, kvol), I32),
            pltpu.SMEM((1,), I32),
            pltpu.VMEM((2 * B, B), BF),
            pltpu.VMEM((kvol, 2 * B, 2 * B), BF),
            pltpu.VMEM((5 * (kvol // 3) * B, 2 * B), BF),
            pltpu.VMEM((wide, 2 * B), BF),
            pltpu.VMEM((2, kvol, B, B), BF),
            pltpu.VMEM((2, B, wide), BF),
            pltpu.VMEM((2, B, wide), BF),
            pltpu.VMEM((B, 2 * B), BF),
            pltpu.VMEM((B, 2 * B), BF),
            pltpu.VMEM((B, 2 * B), F32),
            pltpu.VMEM((2, B, 2 * B), BF),
            pltpu.VMEM((2, 2, B, 2 * B), BF),
            pltpu.VMEM((4, 2, B, 2 * B), BF),
            pltpu.VMEM((2, B, 2 * B), BF),
            pltpu.VMEM((B, B), BF),
            pltpu.VMEM((2, wide + 2 * half - shard, B), F32),
            pltpu.VMEM((2, side, side, half, B), BF),
            pltpu.VMEM((2, side, side, half, B), BF),
            pltpu.VMEM((2, side, side, half, B), BF),
            pltpu.VMEM((2, 2, side // 2, half, B), BF),
            pltpu.VMEM((2, 2, side // 2, half, B), BF),
            pltpu.VMEM((2, 2, side // 2, half, B), BF),
            pltpu.VMEM((2, 2, side // 2, half, B), BF),
            pltpu.VMEM((2, side, half, B), BF),
            pltpu.VMEM((2, side, half, B), BF),
            pltpu.VMEM((2, zside, half, B), BF),
            pltpu.VMEM((2, zside, half, B), BF),
            pltpu.VMEM((2, 2, half, B), F32),
            dma((2,)),
            dma((5,)),
            dma((4, 2)),
            dma((4, 2)),
            dma((2, 3)),
            dma((2, 3)),
            dma((2, 2, 6)),
            dma((2, 2, 6)),
            dma((2, 2, side)),
            dma((2, 2, side)),
            dma((2, zside)),
            dma((2, zside)),
            dma((2, zside)),
            dma((2, zside)),
            dma((2,)),
            dma((2,)),
        ],
        compiler_params=pltpu.CompilerParams(
            collective_id=0, has_side_effects=True, vmem_limit_bytes=67043328
        ),
    )(features, source_rows, target_codes.T, block_count, w1, w2, cot)
    return pl.pallas_call(
        settle,
        out_shape=tuple(jax.ShapeDtypeStruct(r.shape, r.dtype) for r in results),
        in_specs=[vmem] * 4,
        out_specs=(hbm,) * 4,
        scratch_shapes=[dma((4,))],
    )(*results)


def solution(mesh):
    n_grp, n_tile = mesh.shape["grp"], mesh.shape["tile"]
    rows = P(("grp", "tile"), None)
    return jax.shard_map(
        functools.partial(on_device, n_grp, n_tile),
        mesh=mesh,
        in_specs=(
            rows,
            P(None, ("grp", "tile"), None),
            P(None, ("grp", "tile")),
            P(("grp", "tile")),
            P(),
            P(),
            rows,
        ),
        out_specs=(rows, rows, P("grp", None), P("grp", None)),
        check_vma=False,
    )
```

```python
import functools
import math

import jax
import jax.numpy as jnp
from jax import lax
from jax.experimental import pallas as pl
from jax.experimental.pallas import tpu as pltpu
from jax.sharding import PartitionSpec as P

MESH = pl.DeviceIdType.MESH
BF = jnp.bfloat16
F32 = jnp.float32
I32 = jnp.int32
UNROLL = 9


def nn(a, b):
    return lax.dot_general(a, b, (((1,), (0,)), ((), ())), preferred_element_type=F32)


def nt(a, b):
    return lax.dot_general(a, b, (((1,), (1,)), ((), ())), preferred_element_type=F32)


def silu_parts(v):
    s = 1.0 / (1.0 + jnp.exp(-v))
    return v * s, s * (1.0 + v * (1.0 - s))


def kernel(
    dims,
    feat_hbm,
    src_hbm,
    codes_hbm,
    count_hbm,
    w_one,
    w_two,
    cot_hbm,
    out_ref,
    dx_ref,
    wg_one,
    wg_two,
    feat,
    src,
    codes,
    count,
    cot,
    ot,
    pt,
    gt,
    wraw,
    wt,
    wc,
    ht,
    hid,
    pre,
    q,
    xs,
    xr,
    qe,
    hl,
    wgf,
    cs,
    cr,
    sx,
    sf,
    r1,
    r2,
    r3,
    s2,
    r4,
    ab,
    bb,
    fb,
    w_sem,
    i_sem,
    x_send,
    x_recv,
    c_send,
    c_recv,
    g_send,
    g_recv,
    y_send,
    y_recv,
    a_send,
    a_recv,
    b_send,
    b_recv,
    f_send,
    f_recv,
):
    n_grp, n_tile, kvol, rows_k, side, zside = dims
    third = kvol // 3
    B = rows_k
    shard = kvol * B // n_grp
    half = cs.shape[3]
    g = lax.axis_index("grp")
    t = lax.axis_index("tile")
    nz = n_tile // 2
    z = t // 2
    core = t % 2
    gy = g // side
    gx = g % side
    left = lax.rem(t + n_tile - 1, n_tile)
    right = lax.rem(t + 1, n_tile)
    sib = t + 1 - 2 * core
    zlo = z % zside
    zhi = z // zside

    def along(axis, d):
        if axis:
            return gy * side + lax.rem(gx + d, side)
        return lax.rem(gy + d, side) * side + gx

    def near_z(d):
        return (zhi * zside + lax.rem(zlo + d, zside)) * 2 + core

    def far_z(d):
        return (lax.rem(zhi + d, zside) * zside + zlo) * 2 + core

    inputs = [
        pltpu.make_async_copy(a, b, i_sem.at[i])
        for i, (a, b) in enumerate(
            (
                (src_hbm, src),
                (codes_hbm, codes),
                (count_hbm, count),
                (feat_hbm, feat),
                (cot_hbm, cot),
            )
        )
    ]
    for c in inputs[:4]:
        c.start()
    for k, w in ((0, w_one), (1, w_two)):
        pltpu.make_async_copy(w, wraw.at[k], w_sem.at[k]).start()
    inputs[4].start()

    barrier = pltpu.get_barrier_semaphore()
    partners = [{"tile": left}, {"tile": right}]
    partners += [{"grp": along(axis, d)} for axis in range(2) for d in range(1, side)]
    partners += [{"tile": near_z(d)} for d in range(1, zside)]
    partners += [{"tile": far_z(d)} for d in range(1, zside)]
    for p in partners:
        pl.semaphore_signal(barrier, inc=1, device_id=p, device_id_type=MESH)

    for c in inputs[:4]:
        c.wait()
    two = count[0] - 1
    two_f = two.astype(F32)
    one_f = 1.0 - two_f
    keep_prev = jnp.where(t == 0, 0.0, 1.0)
    keep_next = jnp.where(t == n_tile - 1, 0.0, 1.0)

    for j in range(2):
        ht[:, j * B : (j + 1) * B] = feat[j * B : (j + 1) * B, :].T

    def sweep(body):
        def several(i, carry):
            for n in range(UNROLL):
                body(i * UNROLL + n, carry)
            return carry

        lax.fori_loop(0, third // UNROLL, several, 0)

    iota = lax.broadcasted_iota(I32, (B, B), 0)

    def fill(k, at, row, high, live):
        for b in range(2):
            m = (high if b else 1 - high) * live
            idx = row * m + (m - 1)
            hit = jnp.where(iota == idx, 1.0, 0.0).astype(BF)
            ot[k, at : at + B, b * B : (b + 1) * B] = hit

    def entry(k, j):
        return src[k, pl.ds(j, 1), :], codes[j, k] & 1

    def fill_edges(i, carry):
        row, high = entry(3 * i, 0)
        fill(3 * i, 0, row, high, 1)
        k = 3 * i + 2
        row, high = entry(k, 0)
        row_b, high_b = entry(k, 1)
        row = row * (1 - two) + row_b * two
        high = high * (1 - two) + high_b * two
        fill(k, B, row, high, 1)

    def fill_own(i, carry):
        k = 3 * i + 1
        for j in range(2):
            row, high = entry(k, j)
            fill(k, j * B, row, high, two if j else 1)
        row, high = entry(3 * i, 1)
        fill(3 * i, B, row, high, two)
        row, high = entry(3 * i + 2, 0)
        fill(3 * i + 2, 0, row, high, two)

    sweep(fill_edges)

    slots = {1: 0, 0: 1, 2: 2}

    def prep_t(w, classes):
        def body(i, carry):
            for cls in classes:
                at = pl.multiple_of((slots[cls] * third + i) * B, B)
                wt[w, :, pl.ds(at, B)] = wraw[w, 3 * i + cls].T

        sweep(body)

    def prep_c(w):
        def body(i, carry):
            for cls in range(3):
                at = pl.multiple_of((slots[cls] * third + i) * B, B)
                wc[w, :, pl.ds(at, B)] = wraw[w, 3 * i + cls]

        sweep(body)

    def weights_here(w):
        pltpu.make_async_copy(w_two if w else w_one, wraw.at[w], w_sem.at[w]).wait()

    n1 = third * B

    def put(slot, i, value):
        at = pl.multiple_of((slot * third + i) * B, B)
        pt[pl.ds(at, B), :] = value.astype(BF)

    def forward_edges(field, w):
        v = field[:, :B].astype(F32) * one_f + field[:, B:].astype(F32) * two_f
        hl[...] = v.astype(BF)

        def body(i, carry):
            put(3, i, nn(field[:, :B], ot[3 * i, :B, :]))
            put(4, i, nn(hl[...], ot[3 * i + 2, B:, :]))

        sweep(body)
        to_prev = nn(wt[w, :, n1 : 2 * n1], pt[3 * n1 : 4 * n1, :])
        to_next = nn(wt[w, :, 2 * n1 :], pt[4 * n1 :, :])
        xs[w, 0] = to_prev.astype(BF)
        xs[w, 1] = to_next.astype(BF)

    def forward_own(field, w):
        def body(i, carry):
            put(0, i, nn(field[...], ot[3 * i + 1]))
            put(1, i, nn(field[:, B:], ot[3 * i, B:, :]))
            put(2, i, nn(field[:, :B], ot[3 * i + 2, :B, :]))

        sweep(body)
        return nn(wt[w], pt[: 3 * n1, :])

    def exchange(e, to_prev, to_next):
        return [
            pltpu.make_async_remote_copy(
                src_ref=to_prev,
                dst_ref=xr.at[e, 1],
                send_sem=x_send.at[e, 1],
                recv_sem=x_recv.at[e, 1],
                device_id={"tile": left},
                device_id_type=MESH,
            ),
            pltpu.make_async_remote_copy(
                src_ref=to_next,
                dst_ref=xr.at[e, 0],
                send_sem=x_send.at[e, 0],
                recv_sem=x_recv.at[e, 0],
                device_id={"tile": right},
                device_id_type=MESH,
            ),
        ]

    def from_sides(e):
        return (
            xr[e, 0].astype(F32) * keep_prev,
            xr[e, 1].astype(F32) * keep_next,
        )

    def start(copies):
        for c in copies:
            c.start()
        return copies

    def landed(copies):
        for c in copies:
            c.wait_recv()

    pending = []
    mask = jnp.where(
        lax.broadcasted_iota(I32, (1, 2 * B), 1) < B * count[0], 1.0, 0.0
    )

    weights_here(0)
    prep_t(0, (0, 2))
    forward_edges(ht, 0)
    pl.semaphore_wait(barrier, len(partners))
    moved = start(exchange(0, xs.at[0, 0], xs.at[0, 1]))
    pending += moved
    sweep(fill_own)
    prep_t(0, (1,))
    own = forward_own(ht, 0)
    weights_here(1)
    prep_t(1, (0, 1, 2))
    landed(moved)
    before, after = from_sides(0)
    pre_one = own + before + after
    pre[...] = pre_one
    hid[...] = (silu_parts(pre_one)[0] * mask).astype(BF)

    forward_edges(hid, 1)
    moved = start(exchange(1, xs.at[1, 0], xs.at[1, 1]))
    pending += moved
    own = forward_own(hid, 1) + ht[...].astype(F32)
    prep_c(1)
    inputs[4].wait()
    cot_t = jnp.concatenate(
        [cot[:B, :].astype(F32).T, cot[B:, :].astype(F32).T], axis=1
    )
    landed(moved)
    before, after = from_sides(1)
    total = own + before + after
    value, slope = silu_parts(total)
    q[1] = (cot_t * slope * mask).astype(BF)
    moved = start(exchange(2, q.at[1], q.at[1]))
    pending += moved
    result = value * mask
    for j in range(2):
        out_ref[j * B : (j + 1) * B, :] = result[:, j * B : (j + 1) * B].T.astype(BF)

    def put_g(pos, i, lo, hi, v):
        at = pl.multiple_of((pos * third + i) * B, B)
        gt[pl.ds(at, B), lo:hi] = v.astype(BF)

    def back_own(w):
        def body(i, carry):
            put_g(0, i, 0, 2 * B, nt(q[w], ot[3 * i + 1]))
            put_g(1, i, B, 2 * B, nt(q[w], ot[3 * i, B:, :]))
            put_g(2, i, 0, B, nt(q[w], ot[3 * i + 2, :B, :]))

        sweep(body)

    def back_edges(w, e):
        before, after = from_sides(e)
        qe[0] = before.astype(BF)
        qe[1] = after.astype(BF)

        def body(i, carry):
            put_g(1, i, 0, B, nt(qe[0], ot[3 * i, :B, :]))
            last = nt(qe[1], ot[3 * i + 2, B:, :])
            at = pl.multiple_of((2 * third + i) * B, B)
            lower = gt[pl.ds(at, B), :B].astype(F32)
            put_g(2, i, 0, B, lower + last * one_f)
            put_g(2, i, B, 2 * B, last * two_f)

        sweep(body)

    def weight_grads(field, w, classes):
        def body(i, carry):
            for cls in classes:
                at = pl.multiple_of((slots[cls] * third + i) * B, B)
                to = pl.multiple_of((3 * i + cls) * B, B)
                wgf[w, pl.ds(to, B), :] = nt(field[...], gt[pl.ds(at, B), :])

        sweep(body)

    cut = -(-half // 32) * 16
    rows = (pl.ds(0, cut), pl.ds(cut, half - cut))

    def half_rows(w, r, rel, b, h):
        a = lax.rem((gx if r else gy) + rel, side)
        s = b * side + a if r else a * side + b
        at = pl.multiple_of(s * shard + h * half + rows[r].start, 8)
        return wgf[w, pl.ds(at, rows[r].size), :]

    order = (2, 1, 3, 0)
    spans = ((0, 1), (1, 3), (3, 4))

    def send_pair(w):
        copies = []
        for n, (lo, hi) in enumerate(spans):
            for p in range(lo, hi):

                def body(b, carry, p=p):
                    for r in range(2):
                        v = half_rows(w, r, order[p], b, 1 - core)
                        cs[w, p, b, rows[r]] = v.astype(BF)
                    return carry

                lax.fori_loop(0, side, body, 0)
            copies += start(
                [
                    pltpu.make_async_remote_copy(
                        src_ref=cs.at[w, pl.ds(lo, hi - lo)],
                        dst_ref=cr.at[w, pl.ds(lo, hi - lo)],
                        send_sem=c_send.at[w, n],
                        recv_sem=c_recv.at[w, n],
                        device_id={"tile": sib},
                        device_id_type=MESH,
                    )
                ]
            )
        return copies

    def pair_sum(w, p):
        def body(b, carry):
            for r in range(2):
                v = half_rows(w, r, order[p], b, core)
                v = v + cr[w, p, b, rows[r]].astype(F32)
                sx[w, p, b, rows[r]] = v.astype(BF)
            return carry

        lax.fori_loop(0, side, body, 0)

    mid = side // 2
    low, top = pl.ds(0, mid), pl.ds(mid, mid)

    def ring_copy(w, r, n, src_ref, dst_ref, d):
        return pltpu.make_async_remote_copy(
            src_ref=src_ref.at[:, rows[r]],
            dst_ref=dst_ref.at[:, rows[r]],
            send_sem=g_send.at[w, r, n],
            recv_sem=g_recv.at[w, r, n],
            device_id={"grp": along(r, d)},
            device_id_type=MESH,
        )

    def ring_open(w, pair):
        landed(pair[:1])
        pair_sum(w, 0)
        first, second = [], []
        for r in range(2):
            first += start(
                [
                    ring_copy(w, r, 0, sx.at[w, 0, low], r1.at[w, 0], 1),
                    ring_copy(w, r, 1, sx.at[w, 0, top], r1.at[w, 1], side - 1),
                ]
            )
        landed(pair[1:2])
        pair_sum(w, 1)
        pair_sum(w, 2)
        for r in range(2):
            second += start(
                [
                    ring_copy(w, r, 2, sx.at[w, 1, top], r2.at[w, 0], 1),
                    ring_copy(w, r, 3, sx.at[w, 2, low], r2.at[w, 1], side - 1),
                ]
            )
        return first, second

    def ring_close(w, first):
        landed(first)
        third_leg = []
        for n, (p, base, d) in enumerate(((1, 0, 1), (2, mid, side - 1))):

            def body(b, carry, n=n, p=p, base=base):
                v = sx[w, p, base + b].astype(F32) + r1[w, n, b].astype(F32)
                sf[w, n, b] = v.astype(BF)
                return carry

            lax.fori_loop(0, mid, body, 0)
            for r in range(2):
                third_leg += start(
                    [ring_copy(w, r, 4 + n, sf.at[w, n], r3.at[w, n], d)]
                )
        return third_leg

    def cross(w, pair, second, third_leg):
        landed(pair[2:])
        pair_sum(w, 3)
        landed(second)
        landed(third_leg)
        for n in range(2):

            def body(b, carry, n=n):
                v = sx[w, 3, n * mid + b].astype(F32)
                v = v + r3[w, n, b].astype(F32) + r2[w, 1 - n, b].astype(F32)
                s2[w, n * mid + b] = v.astype(BF)
                return carry

            lax.fori_loop(0, mid, body, 0)
        return start(
            [
                pltpu.make_async_remote_copy(
                    src_ref=s2.at[w, lax.rem((gy if r else gx) + d, side), rows[r]],
                    dst_ref=r4.at[w, d, rows[r]],
                    send_sem=y_send.at[w, r, d],
                    recv_sem=y_recv.at[w, r, d],
                    device_id={"grp": along(1 - r, d)},
                    device_id_type=MESH,
                )
                for d in (2, 1, 3)
                for r in range(2)
            ]
        )

    def send_near(w, moved):
        landed(moved)
        for r in range(2):
            acc = s2[w, gy if r else gx, rows[r]].astype(F32)
            for d in range(1, side):
                acc = acc + r4[w, d, rows[r]].astype(F32)
            ab[w, zlo, rows[r]] = acc.astype(BF)
        return start(
            [
                pltpu.make_async_remote_copy(
                    src_ref=ab.at[w, zlo],
                    dst_ref=ab.at[w, zlo],
                    send_sem=a_send.at[w, d],
                    recv_sem=a_recv.at[w, d],
                    device_id={"tile": near_z(d)},
                    device_id_type=MESH,
                )
                for d in range(1, zside)
            ]
        )

    def send_far(w, moved):
        landed(moved)
        acc = ab[w, 0].astype(F32)
        for d in range(1, zside):
            acc = acc + ab[w, d].astype(F32)
        bb[w, zhi] = acc.astype(BF)
        return start(
            [
                pltpu.make_async_remote_copy(
                    src_ref=bb.at[w, zhi],
                    dst_ref=bb.at[w, zhi],
                    send_sem=b_send.at[w, d],
                    recv_sem=b_recv.at[w, d],
                    device_id={"tile": far_z(d)},
                    device_id_type=MESH,
                )
                for d in range(1, zside)
            ]
        )

    def send_last(w, moved):
        landed(moved)
        acc = bb[w, 0].astype(F32)
        for d in range(1, zside):
            acc = acc + bb[w, d].astype(F32)
        fb[w, core] = acc
        return start(
            [
                pltpu.make_async_remote_copy(
                    src_ref=fb.at[w, core],
                    dst_ref=fb.at[w, core],
                    send_sem=f_send.at[w],
                    recv_sem=f_recv.at[w],
                    device_id={"tile": sib},
                    device_id_type=MESH,
                )
            ]
        )

    scale = float(n_grp * n_tile * 2 * B) ** (-0.5)

    def finish(w, moved):
        landed(moved)
        dst = wg_two if w else wg_one
        dst[:half, :] = fb[w, 0] * scale
        dst[half:, :] = fb[w, 1, : shard - half, :] * scale

    for w in range(2 if wgf.shape[1] > kvol * B else 0):
        wgf[w, kvol * B :, :] = jnp.zeros((wgf.shape[1] - kvol * B, B), F32)

    back_own(1)
    landed(moved)
    back_edges(1, 2)
    grad_mid = nn(wc[1], gt[...])
    slope = silu_parts(pre[...])[1]
    q[0] = (grad_mid * slope * mask).astype(BF)
    moved = start(exchange(3, q.at[0], q.at[0]))
    pending += moved
    weight_grads(hid, 1, (0, 1, 2))
    pair_two = send_pair(1)
    back_own(0)
    weight_grads(ht, 0, (1,))
    first_two, second_two = ring_open(1, pair_two)
    landed(moved)
    back_edges(0, 3)
    weight_grads(ht, 0, (0, 2))
    pair_one = send_pair(0)
    third_two = ring_close(1, first_two)
    first_one, second_one = ring_open(0, pair_one)
    cross_two = cross(1, pair_two, second_two, third_two)
    third_one = ring_close(0, first_one)
    prep_c(0)
    grad_in = nn(wc[0], gt[...]) + q[1].astype(F32)
    cross_one = cross(0, pair_one, second_one, third_one)
    near_two = send_near(1, cross_two)
    for j in range(2):
        dx_ref[j * B : (j + 1) * B, :] = grad_in[:, j * B : (j + 1) * B].T.astype(BF)
    near_one = send_near(0, cross_one)
    far_two = send_far(1, near_two)
    far_one = send_far(0, near_one)
    last_two = send_last(1, far_two)
    finish(1, last_two)
    last_one = send_last(0, far_one)
    finish(0, last_one)
    for w in (pair_two, first_two, second_two, third_two, cross_two, near_two):
        pending += w
    for w in (pair_one, first_one, second_one, third_one, cross_one, near_one):
        pending += w
    pending += far_two + far_one + last_two + last_one
    for c in pending:
        c.wait_send()


def settle(*refs):
    sem = refs[8]
    copies = [pltpu.make_async_copy(refs[i], refs[4 + i], sem.at[i]) for i in range(4)]
    for c in copies:
        c.start()
    for c in copies:
        c.wait()


def on_device(n_grp, n_tile, features, source_rows, target_codes, block_count, w1, w2, cot):
    kvol, _, B = source_rows.shape
    side = math.isqrt(n_grp)
    zside = math.isqrt(n_tile // 2)
    shard = kvol * B // n_grp
    half = -(-shard // 32) * 16
    wide = kvol * B
    vmem = pl.BlockSpec(memory_space=pltpu.VMEM)
    hbm = pl.BlockSpec(memory_space=pltpu.HBM)
    dma = pltpu.SemaphoreType.DMA
    dims = (n_grp, n_tile, kvol, B, side, zside)
    held = functools.partial(
        pltpu.with_memory_space_constraint, memory_space=pltpu.HBM
    )
    results = pl.pallas_call(
        functools.partial(kernel, dims),
        out_shape=(
            jax.ShapeDtypeStruct((2 * B, B), BF),
            jax.ShapeDtypeStruct((2 * B, B), BF),
            jax.ShapeDtypeStruct((shard, B), F32),
            jax.ShapeDtypeStruct((shard, B), F32),
        ),
        in_specs=[hbm] * 7,
        out_specs=(vmem,) * 4,
        scratch_shapes=[
            pltpu.VMEM((2 * B, B), BF),
            pltpu.VMEM((kvol, 2, B), I32),
            pltpu.SMEM((2, kvol), I32),
            pltpu.SMEM((1,), I32),
            pltpu.VMEM((2 * B, B), BF),
            pltpu.VMEM((kvol, 2 * B, 2 * B), BF),
            pltpu.VMEM((5 * (kvol // 3) * B, 2 * B), BF),
            pltpu.VMEM((wide, 2 * B), BF),
            pltpu.VMEM((2, kvol, B, B), BF),
            pltpu.VMEM((2, B, wide), BF),
            pltpu.VMEM((2, B, wide), BF),
            pltpu.VMEM((B, 2 * B), BF),
            pltpu.VMEM((B, 2 * B), BF),
            pltpu.VMEM((B, 2 * B), F32),
            pltpu.VMEM((2, B, 2 * B), BF),
            pltpu.VMEM((2, 2, B, 2 * B), BF),
            pltpu.VMEM((4, 2, B, 2 * B), BF),
            pltpu.VMEM((2, B, 2 * B), BF),
            pltpu.VMEM((B, B), BF),
            pltpu.VMEM((2, wide + 2 * half - shard, B), F32),
            pltpu.VMEM((2, side, side, half, B), BF),
            pltpu.VMEM((2, side, side, half, B), BF),
            pltpu.VMEM((2, side, side, half, B), BF),
            pltpu.VMEM((2, 2, side // 2, half, B), BF),
            pltpu.VMEM((2, 2, side // 2, half, B), BF),
            pltpu.VMEM((2, 2, side // 2, half, B), BF),
            pltpu.VMEM((2, 2, side // 2, half, B), BF),
            pltpu.VMEM((2, side, half, B), BF),
            pltpu.VMEM((2, side, half, B), BF),
            pltpu.VMEM((2, zside, half, B), BF),
            pltpu.VMEM((2, zside, half, B), BF),
            pltpu.VMEM((2, 2, half, B), F32),
            dma((2,)),
            dma((5,)),
            dma((4, 2)),
            dma((4, 2)),
            dma((2, 3)),
            dma((2, 3)),
            dma((2, 2, 6)),
            dma((2, 2, 6)),
            dma((2, 2, side)),
            dma((2, 2, side)),
            dma((2, zside)),
            dma((2, zside)),
            dma((2, zside)),
            dma((2, zside)),
            dma((2,)),
            dma((2,)),
        ],
        compiler_params=pltpu.CompilerParams(
            collective_id=0, has_side_effects=True, vmem_limit_bytes=48 * 1024 * 1024
        ),
    )(
        held(features),
        held(source_rows),
        held(target_codes.T),
        block_count,
        held(w1),
        held(w2),
        held(cot),
    )
    return pl.pallas_call(
        settle,
        out_shape=tuple(jax.ShapeDtypeStruct(r.shape, r.dtype) for r in results),
        in_specs=[vmem] * 4,
        out_specs=(hbm,) * 4,
        scratch_shapes=[dma((4,))],
        compiler_params=pltpu.CompilerParams(vmem_limit_bytes=4 * 1024 * 1024),
    )(*results)


def solution(mesh):
    n_grp, n_tile = mesh.shape["grp"], mesh.shape["tile"]
    rows = P(("grp", "tile"), None)
    return jax.shard_map(
        functools.partial(on_device, n_grp, n_tile),
        mesh=mesh,
        in_specs=(
            rows,
            P(None, ("grp", "tile"), None),
            P(None, ("grp", "tile")),
            P(("grp", "tile")),
            P(),
            P(),
            rows,
        ),
        out_specs=(rows, rows, P("grp", None), P("grp", None)),
        check_vma=False,
    )
```

```python
import functools
import math

import jax
import jax.numpy as jnp
from jax import lax
from jax.experimental import pallas as pl
from jax.experimental.pallas import tpu as pltpu
from jax.sharding import PartitionSpec as P

MESH = pl.DeviceIdType.MESH
BF = jnp.bfloat16
F32 = jnp.float32
I32 = jnp.int32
UNROLL = 9


def nn(a, b):
    return lax.dot_general(a, b, (((1,), (0,)), ((), ())), preferred_element_type=F32)


def nt(a, b):
    return lax.dot_general(a, b, (((1,), (1,)), ((), ())), preferred_element_type=F32)


def silu_parts(v):
    s = 1.0 / (1.0 + jnp.exp(-v))
    return v * s, s * (1.0 + v * (1.0 - s))


def kernel(
    dims,
    feat_hbm,
    src_hbm,
    codes_hbm,
    count_hbm,
    w_one,
    w_two,
    cot_hbm,
    out_ref,
    dx_ref,
    wg_one,
    wg_two,
    feat,
    src,
    codes,
    count,
    cot,
    ot,
    pt,
    gt,
    wraw,
    wt,
    wc,
    ht,
    hid,
    pre,
    q,
    xs,
    xr,
    qe,
    hl,
    wgf,
    cs,
    cr,
    sx,
    sf,
    r1,
    r2,
    r3,
    s2,
    r4,
    ab,
    bb,
    fb,
    w_sem,
    i_sem,
    x_send,
    x_recv,
    c_send,
    c_recv,
    g_send,
    g_recv,
    y_send,
    y_recv,
    a_send,
    a_recv,
    b_send,
    b_recv,
    f_send,
    f_recv,
    hello,
):
    n_grp, n_tile, kvol, rows_k, side, zside = dims
    third = kvol // 3
    B = rows_k
    shard = kvol * B // n_grp
    half = cs.shape[3]
    g = lax.axis_index("grp")
    t = lax.axis_index("tile")
    nz = n_tile // 2
    z = t // 2
    core = t % 2
    gy = g // side
    gx = g % side
    left = lax.rem(t + n_tile - 1, n_tile)
    right = lax.rem(t + 1, n_tile)
    sib = t + 1 - 2 * core
    zlo = z % zside
    zhi = z // zside

    def along(axis, d):
        if axis:
            return gy * side + lax.rem(gx + d, side)
        return lax.rem(gy + d, side) * side + gx

    def near_z(d):
        return (zhi * zside + lax.rem(zlo + d, zside)) * 2 + core

    def far_z(d):
        return (lax.rem(zhi + d, zside) * zside + zlo) * 2 + core

    inputs = [
        pltpu.make_async_copy(a, b, i_sem.at[i])
        for i, (a, b) in enumerate(
            (
                (src_hbm, src),
                (codes_hbm, codes),
                (count_hbm, count),
                (feat_hbm, feat),
                (cot_hbm, cot),
            )
        )
    ]
    for c in inputs[:4]:
        c.start()
    for k, w in ((0, w_one), (1, w_two)):
        pltpu.make_async_copy(w, wraw.at[k], w_sem.at[k]).start()
    inputs[4].start()

    barrier = pltpu.get_barrier_semaphore()
    partners = [{"tile": left}, {"tile": right}]
    beside = [{"grp": along(axis, d)} for axis in range(2) for d in (1, side - 1)]
    partners += beside
    for p in partners:
        pl.semaphore_signal(barrier, inc=1, device_id=p, device_id_type=MESH)

    for c in inputs[:4]:
        c.wait()
    def tiles_off(d):
        return [
            {"tile": lax.rem(t + d, n_tile)},
            {"tile": lax.rem(t + n_tile - d, n_tile)},
        ]

    def greet(n, others):
        for p in others:
            pl.semaphore_signal(
                hello.at[n], inc=1, device_id=p, device_id_type=MESH
            )

    two = count[0] - 1
    two_f = two.astype(F32)
    one_f = 1.0 - two_f
    keep_prev = jnp.where(t == 0, 0.0, 1.0)
    keep_next = jnp.where(t == n_tile - 1, 0.0, 1.0)

    for j in range(2):
        ht[:, j * B : (j + 1) * B] = feat[j * B : (j + 1) * B, :].T

    def sweep(body):
        def several(i, carry):
            for n in range(UNROLL):
                body(i * UNROLL + n, carry)
            return carry

        lax.fori_loop(0, third // UNROLL, several, 0)

    iota = lax.broadcasted_iota(I32, (B, B), 0)

    def fill(k, at, row, high, live):
        for b in range(2):
            m = (high if b else 1 - high) * live
            idx = row * m + (m - 1)
            hit = jnp.where(iota == idx, 1.0, 0.0).astype(BF)
            ot[k, at : at + B, b * B : (b + 1) * B] = hit

    def entry(k, j):
        return src[k, pl.ds(j, 1), :], codes[j, k] & 1

    def fill_edges(i, carry):
        row, high = entry(3 * i, 0)
        fill(3 * i, 0, row, high, 1)
        k = 3 * i + 2
        row, high = entry(k, 0)
        row_b, high_b = entry(k, 1)
        row = row * (1 - two) + row_b * two
        high = high * (1 - two) + high_b * two
        fill(k, B, row, high, 1)

    def fill_own(i, carry):
        k = 3 * i + 1
        for j in range(2):
            row, high = entry(k, j)
            fill(k, j * B, row, high, two if j else 1)
        row, high = entry(3 * i, 1)
        fill(3 * i, B, row, high, two)
        row, high = entry(3 * i + 2, 0)
        fill(3 * i + 2, 0, row, high, two)

    sweep(fill_edges)

    slots = {1: 0, 0: 1, 2: 2}

    def prep_t(w, classes):
        def body(i, carry):
            for cls in classes:
                at = pl.multiple_of((slots[cls] * third + i) * B, B)
                wt[w, :, pl.ds(at, B)] = wraw[w, 3 * i + cls].T

        sweep(body)

    def prep_c(w):
        def body(i, carry):
            for cls in range(3):
                at = pl.multiple_of((slots[cls] * third + i) * B, B)
                wc[w, :, pl.ds(at, B)] = wraw[w, 3 * i + cls]

        sweep(body)

    def weights_here(w):
        pltpu.make_async_copy(w_two if w else w_one, wraw.at[w], w_sem.at[w]).wait()

    n1 = third * B

    def put(slot, i, value):
        at = pl.multiple_of((slot * third + i) * B, B)
        pt[pl.ds(at, B), :] = value.astype(BF)

    def forward_edges(field, w):
        v = field[:, :B].astype(F32) * one_f + field[:, B:].astype(F32) * two_f
        hl[...] = v.astype(BF)

        def body(i, carry):
            put(3, i, nn(field[:, :B], ot[3 * i, :B, :]))
            put(4, i, nn(hl[...], ot[3 * i + 2, B:, :]))

        sweep(body)
        to_prev = nn(wt[w, :, n1 : 2 * n1], pt[3 * n1 : 4 * n1, :])
        to_next = nn(wt[w, :, 2 * n1 :], pt[4 * n1 :, :])
        xs[w, 0] = to_prev.astype(BF)
        xs[w, 1] = to_next.astype(BF)

    def forward_own(field, w):
        def body(i, carry):
            put(0, i, nn(field[...], ot[3 * i + 1]))
            put(1, i, nn(field[:, B:], ot[3 * i, B:, :]))
            put(2, i, nn(field[:, :B], ot[3 * i + 2, :B, :]))

        sweep(body)
        return nn(wt[w], pt[: 3 * n1, :])

    def exchange(e, to_prev, to_next):
        return [
            pltpu.make_async_remote_copy(
                src_ref=to_prev,
                dst_ref=xr.at[e, 1],
                send_sem=x_send.at[e, 1],
                recv_sem=x_recv.at[e, 1],
                device_id={"tile": left},
                device_id_type=MESH,
            ),
            pltpu.make_async_remote_copy(
                src_ref=to_next,
                dst_ref=xr.at[e, 0],
                send_sem=x_send.at[e, 0],
                recv_sem=x_recv.at[e, 0],
                device_id={"tile": right},
                device_id_type=MESH,
            ),
        ]

    def from_sides(e):
        return (
            xr[e, 0].astype(F32) * keep_prev,
            xr[e, 1].astype(F32) * keep_next,
        )

    def start(copies):
        for c in copies:
            c.start()
        return copies

    def landed(copies):
        for c in copies:
            c.wait_recv()

    pending = []
    mask = jnp.where(
        lax.broadcasted_iota(I32, (1, 2 * B), 1) < B * count[0], 1.0, 0.0
    )

    weights_here(0)
    prep_t(0, (0, 2))
    forward_edges(ht, 0)
    pl.semaphore_wait(barrier, len(partners))
    greet(0, tiles_off(1))
    greet(1, beside)
    moved = start(exchange(0, xs.at[0, 0], xs.at[0, 1]))
    pending += moved
    sweep(fill_own)
    prep_t(0, (1,))
    own = forward_own(ht, 0)
    weights_here(1)
    prep_t(1, (0, 1, 2))
    landed(moved)
    pl.semaphore_wait(hello.at[0], 2)
    pl.semaphore_wait(hello.at[1], len(beside))
    greet(2, tiles_off(2))
    before, after = from_sides(0)
    pre_one = own + before + after
    pre[...] = pre_one
    hid[...] = (silu_parts(pre_one)[0] * mask).astype(BF)

    forward_edges(hid, 1)
    moved = start(exchange(1, xs.at[1, 0], xs.at[1, 1]))
    pending += moved
    own = forward_own(hid, 1) + ht[...].astype(F32)
    prep_c(1)
    inputs[4].wait()
    cot_t = jnp.concatenate(
        [cot[:B, :].astype(F32).T, cot[B:, :].astype(F32).T], axis=1
    )
    landed(moved)
    pl.semaphore_wait(hello.at[2], 2)
    greet(3, tiles_off(4))
    before, after = from_sides(1)
    total = own + before + after
    value, slope = silu_parts(total)
    q[1] = (cot_t * slope * mask).astype(BF)
    moved = start(exchange(2, q.at[1], q.at[1]))
    pending += moved
    result = value * mask
    for j in range(2):
        out_ref[j * B : (j + 1) * B, :] = result[:, j * B : (j + 1) * B].T.astype(BF)

    def put_g(pos, i, lo, hi, v):
        at = pl.multiple_of((pos * third + i) * B, B)
        gt[pl.ds(at, B), lo:hi] = v.astype(BF)

    def back_own(w):
        def body(i, carry):
            put_g(0, i, 0, 2 * B, nt(q[w], ot[3 * i + 1]))
            put_g(1, i, B, 2 * B, nt(q[w], ot[3 * i, B:, :]))
            put_g(2, i, 0, B, nt(q[w], ot[3 * i + 2, :B, :]))

        sweep(body)

    def back_edges(w, e):
        before, after = from_sides(e)
        qe[0] = before.astype(BF)
        qe[1] = after.astype(BF)

        def body(i, carry):
            put_g(1, i, 0, B, nt(qe[0], ot[3 * i, :B, :]))
            last = nt(qe[1], ot[3 * i + 2, B:, :])
            at = pl.multiple_of((2 * third + i) * B, B)
            lower = gt[pl.ds(at, B), :B].astype(F32)
            put_g(2, i, 0, B, lower + last * one_f)
            put_g(2, i, B, 2 * B, last * two_f)

        sweep(body)

    def weight_grads(field, w, classes):
        def body(i, carry):
            for cls in classes:
                at = pl.multiple_of((slots[cls] * third + i) * B, B)
                to = pl.multiple_of((3 * i + cls) * B, B)
                wgf[w, pl.ds(to, B), :] = nt(field[...], gt[pl.ds(at, B), :])

        sweep(body)

    cut = -(-half // 32) * 16
    rows = (pl.ds(0, cut), pl.ds(cut, half - cut))

    def half_rows(w, r, rel, b, h):
        a = lax.rem((gx if r else gy) + rel, side)
        s = b * side + a if r else a * side + b
        at = pl.multiple_of(s * shard + h * half + rows[r].start, 8)
        return wgf[w, pl.ds(at, rows[r].size), :]

    order = (2, 1, 3, 0)
    spans = ((0, 1), (1, 3), (3, 4))

    def send_pair(w):
        copies = []
        for n, (lo, hi) in enumerate(spans):
            for p in range(lo, hi):

                def body(b, carry, p=p):
                    for r in range(2):
                        v = half_rows(w, r, order[p], b, 1 - core)
                        cs[w, p, b, rows[r]] = v.astype(BF)
                    return carry

                lax.fori_loop(0, side, body, 0)
            copies += start(
                [
                    pltpu.make_async_remote_copy(
                        src_ref=cs.at[w, pl.ds(lo, hi - lo)],
                        dst_ref=cr.at[w, pl.ds(lo, hi - lo)],
                        send_sem=c_send.at[w, n],
                        recv_sem=c_recv.at[w, n],
                        device_id={"tile": sib},
                        device_id_type=MESH,
                    )
                ]
            )
        return copies

    def pair_sum(w, p):
        def body(b, carry):
            for r in range(2):
                v = half_rows(w, r, order[p], b, core)
                v = v + cr[w, p, b, rows[r]].astype(F32)
                sx[w, p, b, rows[r]] = v.astype(BF)
            return carry

        lax.fori_loop(0, side, body, 0)

    mid = side // 2
    low, top = pl.ds(0, mid), pl.ds(mid, mid)

    def ring_copy(w, r, n, src_ref, dst_ref, d):
        return pltpu.make_async_remote_copy(
            src_ref=src_ref.at[:, rows[r]],
            dst_ref=dst_ref.at[:, rows[r]],
            send_sem=g_send.at[w, r, n],
            recv_sem=g_recv.at[w, r, n],
            device_id={"grp": along(r, d)},
            device_id_type=MESH,
        )

    def ring_open(w, pair):
        landed(pair[:1])
        pair_sum(w, 0)
        first, second = [], []
        for r in range(2):
            first += start(
                [
                    ring_copy(w, r, 0, sx.at[w, 0, low], r1.at[w, 0], 1),
                    ring_copy(w, r, 1, sx.at[w, 0, top], r1.at[w, 1], side - 1),
                ]
            )
        landed(pair[1:2])
        pair_sum(w, 1)
        pair_sum(w, 2)
        for r in range(2):
            second += start(
                [
                    ring_copy(w, r, 2, sx.at[w, 1, top], r2.at[w, 0], 1),
                    ring_copy(w, r, 3, sx.at[w, 2, low], r2.at[w, 1], side - 1),
                ]
            )
        return first, second

    def ring_close(w, first):
        landed(first)
        third_leg = []
        for n, (p, base, d) in enumerate(((1, 0, 1), (2, mid, side - 1))):

            def body(b, carry, n=n, p=p, base=base):
                v = sx[w, p, base + b].astype(F32) + r1[w, n, b].astype(F32)
                sf[w, n, b] = v.astype(BF)
                return carry

            lax.fori_loop(0, mid, body, 0)
            for r in range(2):
                third_leg += start(
                    [ring_copy(w, r, 4 + n, sf.at[w, n], r3.at[w, n], d)]
                )
        return third_leg

    def cross(w, pair, second, third_leg):
        landed(pair[2:])
        pair_sum(w, 3)
        landed(second)
        landed(third_leg)
        for n in range(2):

            def body(b, carry, n=n):
                v = sx[w, 3, n * mid + b].astype(F32)
                v = v + r3[w, n, b].astype(F32) + r2[w, 1 - n, b].astype(F32)
                s2[w, n * mid + b] = v.astype(BF)
                return carry

            lax.fori_loop(0, mid, body, 0)
        return start(
            [
                pltpu.make_async_remote_copy(
                    src_ref=s2.at[w, lax.rem((gy if r else gx) + d, side), rows[r]],
                    dst_ref=r4.at[w, d, rows[r]],
                    send_sem=y_send.at[w, r, d],
                    recv_sem=y_recv.at[w, r, d],
                    device_id={"grp": along(1 - r, d)},
                    device_id_type=MESH,
                )
                for d in (2, 1, 3)
                for r in range(2)
            ]
        )

    def send_near(w, moved):
        landed(moved)
        for r in range(2):
            acc = s2[w, gy if r else gx, rows[r]].astype(F32)
            for d in range(1, side):
                acc = acc + r4[w, d, rows[r]].astype(F32)
            ab[w, zlo, rows[r]] = acc.astype(BF)
        return start(
            [
                pltpu.make_async_remote_copy(
                    src_ref=ab.at[w, zlo],
                    dst_ref=ab.at[w, zlo],
                    send_sem=a_send.at[w, d],
                    recv_sem=a_recv.at[w, d],
                    device_id={"tile": near_z(d)},
                    device_id_type=MESH,
                )
                for d in range(1, zside)
            ]
        )

    def send_far(w, moved):
        landed(moved)
        acc = ab[w, 0].astype(F32)
        for d in range(1, zside):
            acc = acc + ab[w, d].astype(F32)
        bb[w, zhi] = acc.astype(BF)
        return start(
            [
                pltpu.make_async_remote_copy(
                    src_ref=bb.at[w, zhi],
                    dst_ref=bb.at[w, zhi],
                    send_sem=b_send.at[w, d],
                    recv_sem=b_recv.at[w, d],
                    device_id={"tile": far_z(d)},
                    device_id_type=MESH,
                )
                for d in range(1, zside)
            ]
        )

    def send_last(w, moved):
        landed(moved)
        acc = bb[w, 0].astype(F32)
        for d in range(1, zside):
            acc = acc + bb[w, d].astype(F32)
        fb[w, core] = acc
        return start(
            [
                pltpu.make_async_remote_copy(
                    src_ref=fb.at[w, core],
                    dst_ref=fb.at[w, core],
                    send_sem=f_send.at[w],
                    recv_sem=f_recv.at[w],
                    device_id={"tile": sib},
                    device_id_type=MESH,
                )
            ]
        )

    scale = float(n_grp * n_tile * 2 * B) ** (-0.5)

    def finish(w, moved):
        landed(moved)
        dst = wg_two if w else wg_one
        dst[:half, :] = fb[w, 0] * scale
        dst[half:, :] = fb[w, 1, : shard - half, :] * scale

    for w in range(2 if wgf.shape[1] > kvol * B else 0):
        wgf[w, kvol * B :, :] = jnp.zeros((wgf.shape[1] - kvol * B, B), F32)

    back_own(1)
    landed(moved)
    pl.semaphore_wait(hello.at[3], 2)
    greet(4, tiles_off(8))
    back_edges(1, 2)
    grad_mid = nn(wc[1], gt[...])
    slope = silu_parts(pre[...])[1]
    q[0] = (grad_mid * slope * mask).astype(BF)
    moved = start(exchange(3, q.at[0], q.at[0]))
    pending += moved
    weight_grads(hid, 1, (0, 1, 2))
    pair_two = send_pair(1)
    back_own(0)
    weight_grads(ht, 0, (1,))
    first_two, second_two = ring_open(1, pair_two)
    landed(moved)
    back_edges(0, 3)
    weight_grads(ht, 0, (0, 2))
    pair_one = send_pair(0)
    third_two = ring_close(1, first_two)
    first_one, second_one = ring_open(0, pair_one)
    cross_two = cross(1, pair_two, second_two, third_two)
    third_one = ring_close(0, first_one)
    prep_c(0)
    grad_in = nn(wc[0], gt[...]) + q[1].astype(F32)
    cross_one = cross(0, pair_one, second_one, third_one)
    near_two = send_near(1, cross_two)
    for j in range(2):
        dx_ref[j * B : (j + 1) * B, :] = grad_in[:, j * B : (j + 1) * B].T.astype(BF)
    near_one = send_near(0, cross_one)
    pl.semaphore_wait(hello.at[4], 2)
    far_two = send_far(1, near_two)
    far_one = send_far(0, near_one)
    last_two = send_last(1, far_two)
    finish(1, last_two)
    last_one = send_last(0, far_one)
    finish(0, last_one)
    for w in (pair_two, first_two, second_two, third_two, cross_two, near_two):
        pending += w
    for w in (pair_one, first_one, second_one, third_one, cross_one, near_one):
        pending += w
    pending += far_two + far_one + last_two + last_one
    for c in pending:
        c.wait_send()


def settle(*refs):
    sem = refs[8]
    copies = [pltpu.make_async_copy(refs[i], refs[4 + i], sem.at[i]) for i in range(4)]
    for c in copies:
        c.start()
    for c in copies:
        c.wait()


def on_device(n_grp, n_tile, features, source_rows, target_codes, block_count, w1, w2, cot):
    kvol, _, B = source_rows.shape
    side = math.isqrt(n_grp)
    zside = math.isqrt(n_tile // 2)
    shard = kvol * B // n_grp
    half = -(-shard // 32) * 16
    wide = kvol * B
    vmem = pl.BlockSpec(memory_space=pltpu.VMEM)
    hbm = pl.BlockSpec(memory_space=pltpu.HBM)
    dma = pltpu.SemaphoreType.DMA
    dims = (n_grp, n_tile, kvol, B, side, zside)
    held = functools.partial(
        pltpu.with_memory_space_constraint, memory_space=pltpu.HBM
    )
    results = pl.pallas_call(
        functools.partial(kernel, dims),
        out_shape=(
            jax.ShapeDtypeStruct((2 * B, B), BF),
            jax.ShapeDtypeStruct((2 * B, B), BF),
            jax.ShapeDtypeStruct((shard, B), F32),
            jax.ShapeDtypeStruct((shard, B), F32),
        ),
        in_specs=[hbm] * 7,
        out_specs=(vmem,) * 4,
        scratch_shapes=[
            pltpu.VMEM((2 * B, B), BF),
            pltpu.VMEM((kvol, 2, B), I32),
            pltpu.SMEM((2, kvol), I32),
            pltpu.SMEM((1,), I32),
            pltpu.VMEM((2 * B, B), BF),
            pltpu.VMEM((kvol, 2 * B, 2 * B), BF),
            pltpu.VMEM((5 * (kvol // 3) * B, 2 * B), BF),
            pltpu.VMEM((wide, 2 * B), BF),
            pltpu.VMEM((2, kvol, B, B), BF),
            pltpu.VMEM((2, B, wide), BF),
            pltpu.VMEM((2, B, wide), BF),
            pltpu.VMEM((B, 2 * B), BF),
            pltpu.VMEM((B, 2 * B), BF),
            pltpu.VMEM((B, 2 * B), F32),
            pltpu.VMEM((2, B, 2 * B), BF),
            pltpu.VMEM((2, 2, B, 2 * B), BF),
            pltpu.VMEM((4, 2, B, 2 * B), BF),
            pltpu.VMEM((2, B, 2 * B), BF),
            pltpu.VMEM((B, B), BF),
            pltpu.VMEM((2, wide + 2 * half - shard, B), F32),
            pltpu.VMEM((2, side, side, half, B), BF),
            pltpu.VMEM((2, side, side, half, B), BF),
            pltpu.VMEM((2, side, side, half, B), BF),
            pltpu.VMEM((2, 2, side // 2, half, B), BF),
            pltpu.VMEM((2, 2, side // 2, half, B), BF),
            pltpu.VMEM((2, 2, side // 2, half, B), BF),
            pltpu.VMEM((2, 2, side // 2, half, B), BF),
            pltpu.VMEM((2, side, half, B), BF),
            pltpu.VMEM((2, side, half, B), BF),
            pltpu.VMEM((2, zside, half, B), BF),
            pltpu.VMEM((2, zside, half, B), BF),
            pltpu.VMEM((2, 2, half, B), F32),
            dma((2,)),
            dma((5,)),
            dma((4, 2)),
            dma((4, 2)),
            dma((2, 3)),
            dma((2, 3)),
            dma((2, 2, 6)),
            dma((2, 2, 6)),
            dma((2, 2, side)),
            dma((2, 2, side)),
            dma((2, zside)),
            dma((2, zside)),
            dma((2, zside)),
            dma((2, zside)),
            dma((2,)),
            dma((2,)),
            pltpu.SemaphoreType.REGULAR((5,)),
        ],
        compiler_params=pltpu.CompilerParams(
            collective_id=0, has_side_effects=True, vmem_limit_bytes=48 * 1024 * 1024
        ),
    )(
        held(features),
        held(source_rows),
        held(target_codes.T),
        block_count,
        held(w1),
        held(w2),
        held(cot),
    )
    return pl.pallas_call(
        settle,
        out_shape=tuple(jax.ShapeDtypeStruct(r.shape, r.dtype) for r in results),
        in_specs=[vmem] * 4,
        out_specs=(hbm,) * 4,
        scratch_shapes=[dma((4,))],
        compiler_params=pltpu.CompilerParams(vmem_limit_bytes=4 * 1024 * 1024),
    )(*results)


def solution(mesh):
    n_grp, n_tile = mesh.shape["grp"], mesh.shape["tile"]
    rows = P(("grp", "tile"), None)
    return jax.shard_map(
        functools.partial(on_device, n_grp, n_tile),
        mesh=mesh,
        in_specs=(
            rows,
            P(None, ("grp", "tile"), None),
            P(None, ("grp", "tile")),
            P(("grp", "tile")),
            P(),
            P(),
            rows,
        ),
        out_specs=(rows, rows, P("grp", None), P("grp", None)),
        check_vma=False,
    )
```

```python
import functools
import math

import jax
import jax.numpy as jnp
from jax import lax
from jax.experimental import pallas as pl
from jax.experimental.pallas import tpu as pltpu
from jax.sharding import PartitionSpec as P

MESH = pl.DeviceIdType.MESH
BF = jnp.bfloat16
F32 = jnp.float32
I32 = jnp.int32
UNROLL = 9


def nn(a, b):
    return lax.dot_general(a, b, (((1,), (0,)), ((), ())), preferred_element_type=F32)


def nt(a, b):
    return lax.dot_general(a, b, (((1,), (1,)), ((), ())), preferred_element_type=F32)


def silu_parts(v):
    s = 1.0 / (1.0 + jnp.exp(-v))
    return v * s, s * (1.0 + v * (1.0 - s))


def kernel(
    dims,
    feat_hbm,
    src_hbm,
    codes_hbm,
    count_hbm,
    w_one,
    w_two,
    cot_hbm,
    out_ref,
    dx_ref,
    wg_one,
    wg_two,
    feat,
    src,
    codes,
    count,
    cot,
    ot,
    pt,
    gt,
    wraw,
    wt,
    wc,
    ht,
    hid,
    pre,
    q,
    xs,
    xr,
    qe,
    hl,
    wgf,
    cs,
    cr,
    sx,
    sf,
    r1,
    r2,
    r3,
    s2,
    r4,
    ab,
    bb,
    fb,
    w_sem,
    i_sem,
    x_send,
    x_recv,
    c_send,
    c_recv,
    g_send,
    g_recv,
    y_send,
    y_recv,
    a_send,
    a_recv,
    b_send,
    b_recv,
    f_send,
    f_recv,
    hello,
):
    n_grp, n_tile, kvol, rows_k, side, zside = dims
    third = kvol // 3
    B = rows_k
    shard = kvol * B // n_grp
    half = cs.shape[3]
    g = lax.axis_index("grp")
    t = lax.axis_index("tile")
    nz = n_tile // 2
    z = t // 2
    core = t % 2
    gy = g // side
    gx = g % side
    left = lax.rem(t + n_tile - 1, n_tile)
    right = lax.rem(t + 1, n_tile)
    sib = t + 1 - 2 * core
    zlo = z % zside
    zhi = z // zside

    def along(axis, d):
        if axis:
            return gy * side + lax.rem(gx + d, side)
        return lax.rem(gy + d, side) * side + gx

    def near_z(d):
        return (zhi * zside + lax.rem(zlo + d, zside)) * 2 + core

    def far_z(d):
        return (lax.rem(zhi + d, zside) * zside + zlo) * 2 + core

    inputs = [
        pltpu.make_async_copy(a, b, i_sem.at[i])
        for i, (a, b) in enumerate(
            (
                (src_hbm, src),
                (codes_hbm, codes),
                (count_hbm, count),
                (feat_hbm, feat),
                (cot_hbm, cot),
            )
        )
    ]
    for c in inputs[:4]:
        c.start()
    for k, w in ((0, w_one), (1, w_two)):
        pltpu.make_async_copy(w, wraw.at[k], w_sem.at[k]).start()
    inputs[4].start()

    barrier = pltpu.get_barrier_semaphore()
    partners = [{"tile": left}, {"tile": right}]
    beside = [{"grp": along(axis, d)} for axis in range(2) for d in (1, side - 1)]
    partners += beside
    for p in partners:
        pl.semaphore_signal(barrier, inc=1, device_id=p, device_id_type=MESH)

    for c in inputs[:4]:
        c.wait()
    def tiles_off(d):
        return [
            {"tile": lax.rem(t + d, n_tile)},
            {"tile": lax.rem(t + n_tile - d, n_tile)},
        ]

    def greet(n, others):
        for p in others:
            pl.semaphore_signal(
                hello.at[n], inc=1, device_id=p, device_id_type=MESH
            )

    two = count[0] - 1
    two_f = two.astype(F32)
    one_f = 1.0 - two_f
    keep_prev = jnp.where(t == 0, 0.0, 1.0)
    keep_next = jnp.where(t == n_tile - 1, 0.0, 1.0)

    for j in range(2):
        ht[:, j * B : (j + 1) * B] = feat[j * B : (j + 1) * B, :].T

    def sweep(body):
        def several(i, carry):
            for n in range(UNROLL):
                body(i * UNROLL + n, carry)
            return carry

        lax.fori_loop(0, third // UNROLL, several, 0)

    iota = lax.broadcasted_iota(I32, (B, B), 0)

    def fill(k, at, row, high, live):
        for b in range(2):
            m = (high if b else 1 - high) * live
            idx = row * m + (m - 1)
            hit = jnp.where(iota == idx, 1.0, 0.0).astype(BF)
            ot[k, at : at + B, b * B : (b + 1) * B] = hit

    def entry(k, j):
        return src[k, pl.ds(j, 1), :], codes[j, k] & 1

    def fill_edges(i, carry):
        row, high = entry(3 * i, 0)
        fill(3 * i, 0, row, high, 1)
        k = 3 * i + 2
        row, high = entry(k, 0)
        row_b, high_b = entry(k, 1)
        row = row * (1 - two) + row_b * two
        high = high * (1 - two) + high_b * two
        fill(k, B, row, high, 1)

    def fill_own(i, carry):
        k = 3 * i + 1
        for j in range(2):
            row, high = entry(k, j)
            fill(k, j * B, row, high, two if j else 1)
        row, high = entry(3 * i, 1)
        fill(3 * i, B, row, high, two)
        row, high = entry(3 * i + 2, 0)
        fill(3 * i + 2, 0, row, high, two)

    sweep(fill_edges)

    slots = {1: 0, 0: 1, 2: 2}

    def prep_t(w, classes):
        def body(i, carry):
            for cls in classes:
                at = pl.multiple_of((slots[cls] * third + i) * B, B)
                wt[w, :, pl.ds(at, B)] = wraw[w, 3 * i + cls].T

        sweep(body)

    def prep_c(w):
        def body(i, carry):
            for cls in range(3):
                at = pl.multiple_of((slots[cls] * third + i) * B, B)
                wc[w, :, pl.ds(at, B)] = wraw[w, 3 * i + cls]

        sweep(body)

    def weights_here(w):
        pltpu.make_async_copy(w_two if w else w_one, wraw.at[w], w_sem.at[w]).wait()

    n1 = third * B

    def put(slot, i, value):
        at = pl.multiple_of((slot * third + i) * B, B)
        pt[pl.ds(at, B), :] = value.astype(BF)

    def forward_edges(field, w):
        v = field[:, :B].astype(F32) * one_f + field[:, B:].astype(F32) * two_f
        hl[...] = v.astype(BF)

        def body(i, carry):
            put(3, i, nn(field[:, :B], ot[3 * i, :B, :]))
            put(4, i, nn(hl[...], ot[3 * i + 2, B:, :]))

        sweep(body)
        to_prev = nn(wt[w, :, n1 : 2 * n1], pt[3 * n1 : 4 * n1, :])
        to_next = nn(wt[w, :, 2 * n1 :], pt[4 * n1 :, :])
        xs[w, 0] = to_prev.astype(BF)
        xs[w, 1] = to_next.astype(BF)

    def forward_own(field, w):
        def body(i, carry):
            put(0, i, nn(field[...], ot[3 * i + 1]))
            put(1, i, nn(field[:, B:], ot[3 * i, B:, :]))
            put(2, i, nn(field[:, :B], ot[3 * i + 2, :B, :]))

        sweep(body)
        return nn(wt[w], pt[: 3 * n1, :])

    def exchange(e, to_prev, to_next):
        return [
            pltpu.make_async_remote_copy(
                src_ref=to_prev,
                dst_ref=xr.at[e, 1],
                send_sem=x_send.at[e, 1],
                recv_sem=x_recv.at[e, 1],
                device_id={"tile": left},
                device_id_type=MESH,
            ),
            pltpu.make_async_remote_copy(
                src_ref=to_next,
                dst_ref=xr.at[e, 0],
                send_sem=x_send.at[e, 0],
                recv_sem=x_recv.at[e, 0],
                device_id={"tile": right},
                device_id_type=MESH,
            ),
        ]

    def from_sides(e):
        return (
            xr[e, 0].astype(F32) * keep_prev,
            xr[e, 1].astype(F32) * keep_next,
        )

    def start(copies):
        for c in copies:
            c.start()
        return copies

    def landed(copies):
        for c in copies:
            c.wait_recv()

    pending = []
    mask = jnp.where(
        lax.broadcasted_iota(I32, (1, 2 * B), 1) < B * count[0], 1.0, 0.0
    )

    weights_here(0)
    prep_t(0, (0, 2))
    forward_edges(ht, 0)
    pl.semaphore_wait(barrier, len(partners))
    greet(0, tiles_off(1))
    greet(1, beside)
    moved = start(exchange(0, xs.at[0, 0], xs.at[0, 1]))
    pending += moved
    sweep(fill_own)
    prep_t(0, (1,))
    own = forward_own(ht, 0)
    weights_here(1)
    prep_t(1, (0, 1, 2))
    landed(moved)
    pl.semaphore_wait(hello.at[0], 2)
    pl.semaphore_wait(hello.at[1], len(beside))
    greet(2, tiles_off(2))
    before, after = from_sides(0)
    pre_one = own + before + after
    pre[...] = pre_one
    hid[...] = (silu_parts(pre_one)[0] * mask).astype(BF)

    forward_edges(hid, 1)
    moved = start(exchange(1, xs.at[1, 0], xs.at[1, 1]))
    pending += moved
    own = forward_own(hid, 1) + ht[...].astype(F32)
    prep_c(1)
    inputs[4].wait()
    cot_t = jnp.concatenate(
        [cot[:B, :].astype(F32).T, cot[B:, :].astype(F32).T], axis=1
    )
    landed(moved)
    pl.semaphore_wait(hello.at[2], 2)
    greet(3, tiles_off(4))
    before, after = from_sides(1)
    total = own + before + after
    value, slope = silu_parts(total)
    q[1] = (cot_t * slope * mask).astype(BF)
    moved = start(exchange(2, q.at[1], q.at[1]))
    pending += moved
    result = value * mask
    for j in range(2):
        out_ref[j * B : (j + 1) * B, :] = result[:, j * B : (j + 1) * B].T.astype(BF)

    def put_g(pos, i, lo, hi, v):
        at = pl.multiple_of((pos * third + i) * B, B)
        gt[pl.ds(at, B), lo:hi] = v.astype(BF)

    def back_own(w):
        def body(i, carry):
            put_g(0, i, 0, 2 * B, nt(q[w], ot[3 * i + 1]))
            put_g(1, i, B, 2 * B, nt(q[w], ot[3 * i, B:, :]))
            put_g(2, i, 0, B, nt(q[w], ot[3 * i + 2, :B, :]))

        sweep(body)

    def back_edges(w, e):
        before, after = from_sides(e)
        qe[0] = before.astype(BF)
        qe[1] = after.astype(BF)

        def body(i, carry):
            put_g(1, i, 0, B, nt(qe[0], ot[3 * i, :B, :]))
            last = nt(qe[1], ot[3 * i + 2, B:, :])
            at = pl.multiple_of((2 * third + i) * B, B)
            lower = gt[pl.ds(at, B), :B].astype(F32)
            put_g(2, i, 0, B, lower + last * one_f)
            put_g(2, i, B, 2 * B, last * two_f)

        sweep(body)

    def weight_grads(field, w, classes):
        def body(i, carry):
            for cls in classes:
                at = pl.multiple_of((slots[cls] * third + i) * B, B)
                to = pl.multiple_of((3 * i + cls) * B, B)
                wgf[w, pl.ds(to, B), :] = nt(field[...], gt[pl.ds(at, B), :])

        sweep(body)

    cut = -(-half // 32) * 16
    rows = (pl.ds(0, cut), pl.ds(cut, half - cut))

    def half_rows(w, r, rel, b, h):
        a = lax.rem((gx if r else gy) + rel, side)
        s = b * side + a if r else a * side + b
        at = pl.multiple_of(s * shard + h * half + rows[r].start, 8)
        return wgf[w, pl.ds(at, rows[r].size), :]

    order = (2, 1, 3, 0)
    spans = ((0, 1), (1, 3), (3, 4))

    def send_pair(w):
        copies = []
        for n, (lo, hi) in enumerate(spans):
            for p in range(lo, hi):

                def body(b, carry, p=p):
                    for r in range(2):
                        v = half_rows(w, r, order[p], b, 1 - core)
                        cs[w, p, b, rows[r]] = v.astype(BF)
                    return carry

                lax.fori_loop(0, side, body, 0)
            copies += start(
                [
                    pltpu.make_async_remote_copy(
                        src_ref=cs.at[w, pl.ds(lo, hi - lo)],
                        dst_ref=cr.at[w, pl.ds(lo, hi - lo)],
                        send_sem=c_send.at[w, n],
                        recv_sem=c_recv.at[w, n],
                        device_id={"tile": sib},
                        device_id_type=MESH,
                    )
                ]
            )
        return copies

    def pair_sum(w, p):
        def body(b, carry):
            for r in range(2):
                v = half_rows(w, r, order[p], b, core)
                v = v + cr[w, p, b, rows[r]].astype(F32)
                sx[w, p, b, rows[r]] = v.astype(BF)
            return carry

        lax.fori_loop(0, side, body, 0)

    mid = side // 2
    low, top = pl.ds(0, mid), pl.ds(mid, mid)

    def ring_copy(w, r, n, src_ref, dst_ref, d):
        return pltpu.make_async_remote_copy(
            src_ref=src_ref.at[:, rows[r]],
            dst_ref=dst_ref.at[:, rows[r]],
            send_sem=g_send.at[w, r, n],
            recv_sem=g_recv.at[w, r, n],
            device_id={"grp": along(r, d)},
            device_id_type=MESH,
        )

    def ring_open(w, pair):
        landed(pair[:1])
        pair_sum(w, 0)
        first, second = [], []
        for r in range(2):
            first += start(
                [
                    ring_copy(w, r, 0, sx.at[w, 0, low], r1.at[w, 0], 1),
                    ring_copy(w, r, 1, sx.at[w, 0, top], r1.at[w, 1], side - 1),
                ]
            )
        landed(pair[1:2])
        pair_sum(w, 1)
        pair_sum(w, 2)
        for r in range(2):
            second += start(
                [
                    ring_copy(w, r, 2, sx.at[w, 1, top], r2.at[w, 0], 1),
                    ring_copy(w, r, 3, sx.at[w, 2, low], r2.at[w, 1], side - 1),
                ]
            )
        return first, second

    def ring_close(w, first):
        landed(first)
        third_leg = []
        for n, (p, base, d) in enumerate(((1, 0, 1), (2, mid, side - 1))):

            def body(b, carry, n=n, p=p, base=base):
                v = sx[w, p, base + b].astype(F32) + r1[w, n, b].astype(F32)
                sf[w, n, b] = v.astype(BF)
                return carry

            lax.fori_loop(0, mid, body, 0)
            for r in range(2):
                third_leg += start(
                    [ring_copy(w, r, 4 + n, sf.at[w, n], r3.at[w, n], d)]
                )
        return third_leg

    def cross(w, pair, second, third_leg):
        landed(pair[2:])
        pair_sum(w, 3)
        landed(second)
        landed(third_leg)
        for n in range(2):

            def body(b, carry, n=n):
                v = sx[w, 3, n * mid + b].astype(F32)
                v = v + r3[w, n, b].astype(F32) + r2[w, 1 - n, b].astype(F32)
                s2[w, n * mid + b] = v.astype(BF)
                return carry

            lax.fori_loop(0, mid, body, 0)
        return start(
            [
                pltpu.make_async_remote_copy(
                    src_ref=s2.at[w, lax.rem((gy if r else gx) + d, side), rows[r]],
                    dst_ref=r4.at[w, d, rows[r]],
                    send_sem=y_send.at[w, r, d],
                    recv_sem=y_recv.at[w, r, d],
                    device_id={"grp": along(1 - r, d)},
                    device_id_type=MESH,
                )
                for d in (2, 1, 3)
                for r in range(2)
            ]
        )

    def send_near(w, moved):
        landed(moved)
        for r in range(2):
            acc = s2[w, gy if r else gx, rows[r]].astype(F32)
            for d in range(1, side):
                acc = acc + r4[w, d, rows[r]].astype(F32)
            ab[w, zlo, rows[r]] = acc.astype(BF)
        return start(
            [
                pltpu.make_async_remote_copy(
                    src_ref=ab.at[w, zlo],
                    dst_ref=ab.at[w, zlo],
                    send_sem=a_send.at[w, d],
                    recv_sem=a_recv.at[w, d],
                    device_id={"tile": near_z(d)},
                    device_id_type=MESH,
                )
                for d in range(1, zside)
            ]
        )

    def send_far(w, moved):
        landed(moved)
        acc = ab[w, 0].astype(F32)
        for d in range(1, zside):
            acc = acc + ab[w, d].astype(F32)
        bb[w, zhi] = acc.astype(BF)
        return start(
            [
                pltpu.make_async_remote_copy(
                    src_ref=bb.at[w, zhi],
                    dst_ref=bb.at[w, zhi],
                    send_sem=b_send.at[w, d],
                    recv_sem=b_recv.at[w, d],
                    device_id={"tile": far_z(d)},
                    device_id_type=MESH,
                )
                for d in (2, 1, 3)
            ]
        )

    def send_last(w, moved):
        landed(moved)
        acc = bb[w, 0].astype(F32)
        for d in range(1, zside):
            acc = acc + bb[w, d].astype(F32)
        fb[w, core] = acc
        return start(
            [
                pltpu.make_async_remote_copy(
                    src_ref=fb.at[w, core],
                    dst_ref=fb.at[w, core],
                    send_sem=f_send.at[w],
                    recv_sem=f_recv.at[w],
                    device_id={"tile": sib},
                    device_id_type=MESH,
                )
            ]
        )

    scale = float(n_grp * n_tile * 2 * B) ** (-0.5)

    def finish(w, moved):
        landed(moved)
        dst = wg_two if w else wg_one
        dst[:half, :] = fb[w, 0] * scale
        dst[half:, :] = fb[w, 1, : shard - half, :] * scale

    for w in range(2 if wgf.shape[1] > kvol * B else 0):
        wgf[w, kvol * B :, :] = jnp.zeros((wgf.shape[1] - kvol * B, B), F32)

    back_own(1)
    grad_mid = nn(wc[1, :, :n1], gt[:n1, :])
    weight_grads(hid, 1, (1,))
    landed(moved)
    pl.semaphore_wait(hello.at[3], 2)
    greet(4, tiles_off(8))
    back_edges(1, 2)
    grad_mid = grad_mid + nn(wc[1, :, n1:], gt[n1:, :])
    slope = silu_parts(pre[...])[1]
    q[0] = (grad_mid * slope * mask).astype(BF)
    moved = start(exchange(3, q.at[0], q.at[0]))
    pending += moved
    weight_grads(hid, 1, (0, 2))
    pair_two = send_pair(1)
    back_own(0)
    weight_grads(ht, 0, (1,))
    first_two, second_two = ring_open(1, pair_two)
    landed(moved)
    back_edges(0, 3)
    weight_grads(ht, 0, (0, 2))
    pair_one = send_pair(0)
    third_two = ring_close(1, first_two)
    first_one, second_one = ring_open(0, pair_one)
    cross_two = cross(1, pair_two, second_two, third_two)
    third_one = ring_close(0, first_one)
    prep_c(0)
    grad_in = nn(wc[0], gt[...]) + q[1].astype(F32)
    cross_one = cross(0, pair_one, second_one, third_one)
    near_two = send_near(1, cross_two)
    for j in range(2):
        dx_ref[j * B : (j + 1) * B, :] = grad_in[:, j * B : (j + 1) * B].T.astype(BF)
    near_one = send_near(0, cross_one)
    pl.semaphore_wait(hello.at[4], 2)
    far_two = send_far(1, near_two)
    far_one = send_far(0, near_one)
    last_two = send_last(1, far_two)
    last_one = send_last(0, far_one)
    finish(1, last_two)
    finish(0, last_one)
    for w in (pair_two, first_two, second_two, third_two, cross_two, near_two):
        pending += w
    for w in (pair_one, first_one, second_one, third_one, cross_one, near_one):
        pending += w
    pending += far_two + far_one + last_two + last_one
    for c in pending:
        c.wait_send()


def settle(*refs):
    sem = refs[8]
    copies = [pltpu.make_async_copy(refs[i], refs[4 + i], sem.at[i]) for i in range(4)]
    for c in copies:
        c.start()
    for c in copies:
        c.wait()


def on_device(n_grp, n_tile, features, source_rows, target_codes, block_count, w1, w2, cot):
    kvol, _, B = source_rows.shape
    side = math.isqrt(n_grp)
    zside = math.isqrt(n_tile // 2)
    shard = kvol * B // n_grp
    half = -(-shard // 32) * 16
    wide = kvol * B
    vmem = pl.BlockSpec(memory_space=pltpu.VMEM)
    hbm = pl.BlockSpec(memory_space=pltpu.HBM)
    dma = pltpu.SemaphoreType.DMA
    dims = (n_grp, n_tile, kvol, B, side, zside)
    held = functools.partial(
        pltpu.with_memory_space_constraint, memory_space=pltpu.HBM
    )
    results = pl.pallas_call(
        functools.partial(kernel, dims),
        out_shape=(
            jax.ShapeDtypeStruct((2 * B, B), BF),
            jax.ShapeDtypeStruct((2 * B, B), BF),
            jax.ShapeDtypeStruct((shard, B), F32),
            jax.ShapeDtypeStruct((shard, B), F32),
        ),
        in_specs=[hbm] * 7,
        out_specs=(vmem,) * 4,
        scratch_shapes=[
            pltpu.VMEM((2 * B, B), BF),
            pltpu.VMEM((kvol, 2, B), I32),
            pltpu.SMEM((2, kvol), I32),
            pltpu.SMEM((1,), I32),
            pltpu.VMEM((2 * B, B), BF),
            pltpu.VMEM((kvol, 2 * B, 2 * B), BF),
            pltpu.VMEM((5 * (kvol // 3) * B, 2 * B), BF),
            pltpu.VMEM((wide, 2 * B), BF),
            pltpu.VMEM((2, kvol, B, B), BF),
            pltpu.VMEM((2, B, wide), BF),
            pltpu.VMEM((2, B, wide), BF),
            pltpu.VMEM((B, 2 * B), BF),
            pltpu.VMEM((B, 2 * B), BF),
            pltpu.VMEM((B, 2 * B), F32),
            pltpu.VMEM((2, B, 2 * B), BF),
            pltpu.VMEM((2, 2, B, 2 * B), BF),
            pltpu.VMEM((4, 2, B, 2 * B), BF),
            pltpu.VMEM((2, B, 2 * B), BF),
            pltpu.VMEM((B, B), BF),
            pltpu.VMEM((2, wide + 2 * half - shard, B), F32),
            pltpu.VMEM((2, side, side, half, B), BF),
            pltpu.VMEM((2, side, side, half, B), BF),
            pltpu.VMEM((2, side, side, half, B), BF),
            pltpu.VMEM((2, 2, side // 2, half, B), BF),
            pltpu.VMEM((2, 2, side // 2, half, B), BF),
            pltpu.VMEM((2, 2, side // 2, half, B), BF),
            pltpu.VMEM((2, 2, side // 2, half, B), BF),
            pltpu.VMEM((2, side, half, B), BF),
            pltpu.VMEM((2, side, half, B), BF),
            pltpu.VMEM((2, zside, half, B), BF),
            pltpu.VMEM((2, zside, half, B), BF),
            pltpu.VMEM((2, 2, half, B), F32),
            dma((2,)),
            dma((5,)),
            dma((4, 2)),
            dma((4, 2)),
            dma((2, 3)),
            dma((2, 3)),
            dma((2, 2, 6)),
            dma((2, 2, 6)),
            dma((2, 2, side)),
            dma((2, 2, side)),
            dma((2, zside)),
            dma((2, zside)),
            dma((2, zside)),
            dma((2, zside)),
            dma((2,)),
            dma((2,)),
            pltpu.SemaphoreType.REGULAR((5,)),
        ],
        compiler_params=pltpu.CompilerParams(
            collective_id=0, has_side_effects=True, vmem_limit_bytes=48 * 1024 * 1024
        ),
    )(
        held(features),
        held(source_rows),
        held(target_codes.T),
        block_count,
        held(w1),
        held(w2),
        held(cot),
    )
    return pl.pallas_call(
        settle,
        out_shape=tuple(jax.ShapeDtypeStruct(r.shape, r.dtype) for r in results),
        in_specs=[vmem] * 4,
        out_specs=(hbm,) * 4,
        scratch_shapes=[dma((4,))],
        compiler_params=pltpu.CompilerParams(vmem_limit_bytes=4 * 1024 * 1024),
    )(*results)


def solution(mesh):
    n_grp, n_tile = mesh.shape["grp"], mesh.shape["tile"]
    rows = P(("grp", "tile"), None)
    return jax.shard_map(
        functools.partial(on_device, n_grp, n_tile),
        mesh=mesh,
        in_specs=(
            rows,
            P(None, ("grp", "tile"), None),
            P(None, ("grp", "tile")),
            P(("grp", "tile")),
            P(),
            P(),
            rows,
        ),
        out_specs=(rows, rows, P("grp", None), P("grp", None)),
        check_vma=False,
    )
```

```python
import functools
import math

import jax
import jax.numpy as jnp
from jax import lax
from jax.experimental import pallas as pl
from jax.experimental.pallas import tpu as pltpu
from jax.sharding import PartitionSpec as P

MESH = pl.DeviceIdType.MESH
BF = jnp.bfloat16
F32 = jnp.float32
I32 = jnp.int32
UNROLL = 9


def nn(a, b):
    return lax.dot_general(a, b, (((1,), (0,)), ((), ())), preferred_element_type=F32)


def nt(a, b):
    return lax.dot_general(a, b, (((1,), (1,)), ((), ())), preferred_element_type=F32)


def silu_parts(v):
    s = 1.0 / (1.0 + jnp.exp(-v))
    return v * s, s * (1.0 + v * (1.0 - s))


def kernel(
    dims,
    feat_hbm,
    src_hbm,
    codes_hbm,
    count_hbm,
    w_one,
    w_two,
    cot_hbm,
    out_ref,
    dx_ref,
    wg_one,
    wg_two,
    feat,
    src,
    codes,
    count,
    cot,
    ot,
    pt,
    gt,
    wraw,
    wt,
    wc,
    ht,
    hid,
    pre,
    q,
    xs,
    xr,
    qe,
    hl,
    wgf,
    cs,
    cr,
    sx,
    sf,
    r1,
    r2,
    r3,
    s2,
    r4,
    ab,
    bb,
    fb,
    w_sem,
    i_sem,
    x_send,
    x_recv,
    c_send,
    c_recv,
    g_send,
    g_recv,
    y_send,
    y_recv,
    a_send,
    a_recv,
    b_send,
    b_recv,
    f_send,
    f_recv,
    hello,
):
    n_grp, n_tile, kvol, rows_k, side, zside = dims
    third = kvol // 3
    B = rows_k
    shard = kvol * B // n_grp
    half = cs.shape[3]
    g = lax.axis_index("grp")
    t = lax.axis_index("tile")
    nz = n_tile // 2
    z = t // 2
    core = t % 2
    gy = g // side
    gx = g % side
    left = lax.rem(t + n_tile - 1, n_tile)
    right = lax.rem(t + 1, n_tile)
    sib = t + 1 - 2 * core
    zlo = z % zside
    zhi = z // zside

    def along(axis, d):
        if axis:
            return gy * side + lax.rem(gx + d, side)
        return lax.rem(gy + d, side) * side + gx

    def near_z(d):
        return (zhi * zside + lax.rem(zlo + d, zside)) * 2 + core

    def far_z(d):
        return (lax.rem(zhi + d, zside) * zside + zlo) * 2 + core

    inputs = [
        pltpu.make_async_copy(a, b, i_sem.at[i])
        for i, (a, b) in enumerate(
            (
                (src_hbm, src),
                (codes_hbm, codes),
                (count_hbm, count),
                (feat_hbm, feat),
                (cot_hbm, cot),
            )
        )
    ]
    for c in inputs[:4]:
        c.start()
    for k, w in ((0, w_one), (1, w_two)):
        pltpu.make_async_copy(w, wraw.at[k], w_sem.at[k]).start()
    inputs[4].start()

    barrier = pltpu.get_barrier_semaphore()
    partners = [{"tile": left}, {"tile": right}]
    beside = [{"grp": along(axis, d)} for axis in range(2) for d in (1, side - 1)]
    partners += beside
    for p in partners:
        pl.semaphore_signal(barrier, inc=1, device_id=p, device_id_type=MESH)

    for c in inputs[:4]:
        c.wait()
    def tiles_off(d):
        return [
            {"tile": lax.rem(t + d, n_tile)},
            {"tile": lax.rem(t + n_tile - d, n_tile)},
        ]

    def greet(n, others):
        for p in others:
            pl.semaphore_signal(
                hello.at[n], inc=1, device_id=p, device_id_type=MESH
            )

    two = count[0] - 1
    two_f = two.astype(F32)
    one_f = 1.0 - two_f
    keep_prev = jnp.where(t == 0, 0.0, 1.0)
    keep_next = jnp.where(t == n_tile - 1, 0.0, 1.0)

    for j in range(2):
        ht[:, j * B : (j + 1) * B] = feat[j * B : (j + 1) * B, :].T

    def sweep(body):
        def several(i, carry):
            for n in range(UNROLL):
                body(i * UNROLL + n, carry)
            return carry

        lax.fori_loop(0, third // UNROLL, several, 0)

    iota = lax.broadcasted_iota(I32, (B, B), 0)

    def fill(k, at, row, high, live):
        for b in range(2):
            m = (high if b else 1 - high) * live
            idx = row * m + (m - 1)
            hit = jnp.where(iota == idx, 1.0, 0.0).astype(BF)
            ot[k, at : at + B, b * B : (b + 1) * B] = hit

    def entry(k, j):
        return src[k, pl.ds(j, 1), :], codes[j, k] & 1

    def fill_edges(i, carry):
        row, high = entry(3 * i, 0)
        fill(3 * i, 0, row, high, 1)
        k = 3 * i + 2
        row, high = entry(k, 0)
        row_b, high_b = entry(k, 1)
        row = row * (1 - two) + row_b * two
        high = high * (1 - two) + high_b * two
        fill(k, B, row, high, 1)

    def fill_own(i, carry):
        k = 3 * i + 1
        for j in range(2):
            row, high = entry(k, j)
            fill(k, j * B, row, high, two if j else 1)
        row, high = entry(3 * i, 1)
        fill(3 * i, B, row, high, two)
        row, high = entry(3 * i + 2, 0)
        fill(3 * i + 2, 0, row, high, two)

    sweep(fill_edges)

    slots = {1: 0, 0: 1, 2: 2}

    def prep_t(w, classes):
        def body(i, carry):
            for cls in classes:
                at = pl.multiple_of((slots[cls] * third + i) * B, B)
                wt[w, :, pl.ds(at, B)] = wraw[w, 3 * i + cls].T

        sweep(body)

    def prep_c(w):
        def body(i, carry):
            for cls in range(3):
                at = pl.multiple_of((slots[cls] * third + i) * B, B)
                wc[w, :, pl.ds(at, B)] = wraw[w, 3 * i + cls]

        sweep(body)

    def weights_here(w):
        pltpu.make_async_copy(w_two if w else w_one, wraw.at[w], w_sem.at[w]).wait()

    n1 = third * B

    def put(slot, i, value):
        at = pl.multiple_of((slot * third + i) * B, B)
        pt[pl.ds(at, B), :] = value.astype(BF)

    def forward_edges(field, w):
        v = field[:, :B].astype(F32) * one_f + field[:, B:].astype(F32) * two_f
        hl[...] = v.astype(BF)

        def body(i, carry):
            put(3, i, nn(field[:, :B], ot[3 * i, :B, :]))
            put(4, i, nn(hl[...], ot[3 * i + 2, B:, :]))

        sweep(body)
        to_prev = nn(wt[w, :, n1 : 2 * n1], pt[3 * n1 : 4 * n1, :])
        to_next = nn(wt[w, :, 2 * n1 :], pt[4 * n1 :, :])
        xs[w, 0] = to_prev.astype(BF)
        xs[w, 1] = to_next.astype(BF)

    def forward_own(field, w):
        def body(i, carry):
            put(0, i, nn(field[...], ot[3 * i + 1]))
            put(1, i, nn(field[:, B:], ot[3 * i, B:, :]))
            put(2, i, nn(field[:, :B], ot[3 * i + 2, :B, :]))

        sweep(body)
        return nn(wt[w], pt[: 3 * n1, :])

    def exchange(e, to_prev, to_next):
        return [
            pltpu.make_async_remote_copy(
                src_ref=to_prev,
                dst_ref=xr.at[e, 1],
                send_sem=x_send.at[e, 1],
                recv_sem=x_recv.at[e, 1],
                device_id={"tile": left},
                device_id_type=MESH,
            ),
            pltpu.make_async_remote_copy(
                src_ref=to_next,
                dst_ref=xr.at[e, 0],
                send_sem=x_send.at[e, 0],
                recv_sem=x_recv.at[e, 0],
                device_id={"tile": right},
                device_id_type=MESH,
            ),
        ]

    def from_sides(e):
        return (
            xr[e, 0].astype(F32) * keep_prev,
            xr[e, 1].astype(F32) * keep_next,
        )

    def start(copies):
        for c in copies:
            c.start()
        return copies

    def landed(copies):
        for c in copies:
            c.wait_recv()

    pending = []
    mask = jnp.where(
        lax.broadcasted_iota(I32, (1, 2 * B), 1) < B * count[0], 1.0, 0.0
    )

    weights_here(0)
    prep_t(0, (0, 2))
    forward_edges(ht, 0)
    pl.semaphore_wait(barrier, len(partners))
    greet(0, tiles_off(1))
    greet(1, beside)
    moved = start(exchange(0, xs.at[0, 0], xs.at[0, 1]))
    pending += moved
    sweep(fill_own)
    prep_t(0, (1,))
    own = forward_own(ht, 0)
    weights_here(1)
    prep_t(1, (0, 1, 2))
    landed(moved)
    pl.semaphore_wait(hello.at[0], 2)
    pl.semaphore_wait(hello.at[1], len(beside))
    greet(2, tiles_off(2))
    before, after = from_sides(0)
    pre_one = own + before + after
    pre[...] = pre_one
    hid[...] = (silu_parts(pre_one)[0] * mask).astype(BF)

    forward_edges(hid, 1)
    moved = start(exchange(1, xs.at[1, 0], xs.at[1, 1]))
    pending += moved
    own = forward_own(hid, 1) + ht[...].astype(F32)
    prep_c(1)
    inputs[4].wait()
    cot_t = jnp.concatenate(
        [cot[:B, :].astype(F32).T, cot[B:, :].astype(F32).T], axis=1
    )
    landed(moved)
    pl.semaphore_wait(hello.at[2], 2)
    greet(3, tiles_off(4))
    before, after = from_sides(1)
    total = own + before + after
    value, slope = silu_parts(total)
    q[1] = (cot_t * slope * mask).astype(BF)
    moved = start(exchange(2, q.at[1], q.at[1]))
    pending += moved
    result = value * mask
    for j in range(2):
        out_ref[j * B : (j + 1) * B, :] = result[:, j * B : (j + 1) * B].T.astype(BF)

    def put_g(pos, i, lo, hi, v):
        at = pl.multiple_of((pos * third + i) * B, B)
        gt[pl.ds(at, B), lo:hi] = v.astype(BF)

    def back_own(w):
        def body(i, carry):
            put_g(0, i, 0, 2 * B, nt(q[w], ot[3 * i + 1]))
            put_g(1, i, B, 2 * B, nt(q[w], ot[3 * i, B:, :]))
            put_g(2, i, 0, B, nt(q[w], ot[3 * i + 2, :B, :]))

        sweep(body)

    def back_edges(w, e):
        before, after = from_sides(e)
        qe[0] = before.astype(BF)
        qe[1] = after.astype(BF)

        def body(i, carry):
            put_g(1, i, 0, B, nt(qe[0], ot[3 * i, :B, :]))
            last = nt(qe[1], ot[3 * i + 2, B:, :])
            at = pl.multiple_of((2 * third + i) * B, B)
            lower = gt[pl.ds(at, B), :B].astype(F32)
            put_g(2, i, 0, B, lower + last * one_f)
            put_g(2, i, B, 2 * B, last * two_f)

        sweep(body)

    def weight_grads(field, w, classes):
        def body(i, carry):
            for cls in classes:
                at = pl.multiple_of((slots[cls] * third + i) * B, B)
                to = pl.multiple_of((3 * i + cls) * B, B)
                wgf[w, pl.ds(to, B), :] = nt(field[...], gt[pl.ds(at, B), :])

        sweep(body)

    cut = -(-half // 32) * 16
    rows = (pl.ds(0, cut), pl.ds(cut, half - cut))

    def half_rows(w, r, rel, b, h):
        a = lax.rem((gx if r else gy) + rel, side)
        s = b * side + a if r else a * side + b
        at = pl.multiple_of(s * shard + h * half + rows[r].start, 8)
        return wgf[w, pl.ds(at, rows[r].size), :]

    order = (2, 1, 3, 0)
    spans = ((0, 1), (1, 3), (3, 4))

    def send_pair(w):
        copies = []
        for n, (lo, hi) in enumerate(spans):
            for p in range(lo, hi):

                def body(b, carry, p=p):
                    for r in range(2):
                        v = half_rows(w, r, order[p], b, 1 - core)
                        cs[w, p, b, rows[r]] = v.astype(BF)
                    return carry

                lax.fori_loop(0, side, body, 0)
            copies += start(
                [
                    pltpu.make_async_remote_copy(
                        src_ref=cs.at[w, pl.ds(lo, hi - lo)],
                        dst_ref=cr.at[w, pl.ds(lo, hi - lo)],
                        send_sem=c_send.at[w, n],
                        recv_sem=c_recv.at[w, n],
                        device_id={"tile": sib},
                        device_id_type=MESH,
                    )
                ]
            )
        return copies

    def pair_sum(w, p):
        def body(b, carry):
            for r in range(2):
                v = half_rows(w, r, order[p], b, core)
                v = v + cr[w, p, b, rows[r]].astype(F32)
                sx[w, p, b, rows[r]] = v.astype(BF)
            return carry

        lax.fori_loop(0, side, body, 0)

    mid = side // 2
    low, top = pl.ds(0, mid), pl.ds(mid, mid)

    def ring_copy(w, r, n, src_ref, dst_ref, d):
        return pltpu.make_async_remote_copy(
            src_ref=src_ref.at[:, rows[r]],
            dst_ref=dst_ref.at[:, rows[r]],
            send_sem=g_send.at[w, r, n],
            recv_sem=g_recv.at[w, r, n],
            device_id={"grp": along(r, d)},
            device_id_type=MESH,
        )

    def ring_open(w, pair):
        landed(pair[:1])
        pair_sum(w, 0)
        first, second = [], []
        for r in range(2):
            first += start(
                [
                    ring_copy(w, r, 0, sx.at[w, 0, low], r1.at[w, 0], 1),
                    ring_copy(w, r, 1, sx.at[w, 0, top], r1.at[w, 1], side - 1),
                ]
            )
        landed(pair[1:2])
        pair_sum(w, 1)
        pair_sum(w, 2)
        for r in range(2):
            second += start(
                [
                    ring_copy(w, r, 2, sx.at[w, 1, top], r2.at[w, 0], 1),
                    ring_copy(w, r, 3, sx.at[w, 2, low], r2.at[w, 1], side - 1),
                ]
            )
        return first, second

    def ring_close(w, first):
        landed(first)
        third_leg = []
        for n, (p, base, d) in enumerate(((1, 0, 1), (2, mid, side - 1))):

            def body(b, carry, n=n, p=p, base=base):
                v = sx[w, p, base + b].astype(F32) + r1[w, n, b].astype(F32)
                sf[w, n, b] = v.astype(BF)
                return carry

            lax.fori_loop(0, mid, body, 0)
            for r in range(2):
                third_leg += start(
                    [ring_copy(w, r, 4 + n, sf.at[w, n], r3.at[w, n], d)]
                )
        return third_leg

    def cross(w, pair, second, third_leg):
        landed(pair[2:])
        pair_sum(w, 3)
        landed(second)
        landed(third_leg)
        for n in range(2):

            def body(b, carry, n=n):
                v = sx[w, 3, n * mid + b].astype(F32)
                v = v + r3[w, n, b].astype(F32) + r2[w, 1 - n, b].astype(F32)
                s2[w, n * mid + b] = v.astype(BF)
                return carry

            lax.fori_loop(0, mid, body, 0)
        return start(
            [
                pltpu.make_async_remote_copy(
                    src_ref=s2.at[w, lax.rem((gy if r else gx) + d, side), rows[r]],
                    dst_ref=r4.at[w, d, rows[r]],
                    send_sem=y_send.at[w, r, d],
                    recv_sem=y_recv.at[w, r, d],
                    device_id={"grp": along(1 - r, d)},
                    device_id_type=MESH,
                )
                for d in (2, 1, 3)
                for r in range(2)
            ]
        )

    def send_near(w, moved):
        landed(moved)
        for r in range(2):
            acc = s2[w, gy if r else gx, rows[r]].astype(F32)
            for d in range(1, side):
                acc = acc + r4[w, d, rows[r]].astype(F32)
            ab[w, zlo, rows[r]] = acc.astype(BF)
        return start(
            [
                pltpu.make_async_remote_copy(
                    src_ref=ab.at[w, zlo],
                    dst_ref=ab.at[w, zlo],
                    send_sem=a_send.at[w, d],
                    recv_sem=a_recv.at[w, d],
                    device_id={"tile": near_z(d)},
                    device_id_type=MESH,
                )
                for d in range(1, zside)
            ]
        )

    def send_far(w, moved):
        landed(moved)
        acc = ab[w, 0].astype(F32)
        for d in range(1, zside):
            acc = acc + ab[w, d].astype(F32)
        bb[w, zhi] = acc.astype(BF)
        return start(
            [
                pltpu.make_async_remote_copy(
                    src_ref=bb.at[w, zhi],
                    dst_ref=bb.at[w, zhi],
                    send_sem=b_send.at[w, d],
                    recv_sem=b_recv.at[w, d],
                    device_id={"tile": far_z(d)},
                    device_id_type=MESH,
                )
                for d in (2, 1, 3)
            ]
        )

    def send_last(w, moved):
        landed(moved)
        acc = bb[w, 0].astype(F32)
        for d in range(1, zside):
            acc = acc + bb[w, d].astype(F32)
        fb[w, core] = acc
        return start(
            [
                pltpu.make_async_remote_copy(
                    src_ref=fb.at[w, core],
                    dst_ref=fb.at[w, core],
                    send_sem=f_send.at[w],
                    recv_sem=f_recv.at[w],
                    device_id={"tile": sib},
                    device_id_type=MESH,
                )
            ]
        )

    scale = float(n_grp * n_tile * 2 * B) ** (-0.5)

    def finish(w, moved):
        landed(moved)
        dst = wg_two if w else wg_one
        dst[:half, :] = fb[w, 0] * scale
        dst[half:, :] = fb[w, 1, : shard - half, :] * scale

    for w in range(2 if wgf.shape[1] > kvol * B else 0):
        wgf[w, kvol * B :, :] = jnp.zeros((wgf.shape[1] - kvol * B, B), F32)

    back_own(1)
    grad_mid = nn(wc[1, :, :n1], gt[:n1, :])
    weight_grads(hid, 1, (1,))
    landed(moved)
    pl.semaphore_wait(hello.at[3], 2)
    greet(4, tiles_off(8))
    back_edges(1, 2)
    grad_mid = grad_mid + nn(wc[1, :, n1:], gt[n1:, :])
    slope = silu_parts(pre[...])[1]
    q[0] = (grad_mid * slope * mask).astype(BF)
    moved = start(exchange(3, q.at[0], q.at[0]))
    pending += moved
    weight_grads(hid, 1, (0, 2))
    pair_two = send_pair(1)
    back_own(0)
    weight_grads(ht, 0, (1,))
    first_two, second_two = ring_open(1, pair_two)
    landed(moved)
    back_edges(0, 3)
    weight_grads(ht, 0, (0, 2))
    pair_one = send_pair(0)
    third_two = ring_close(1, first_two)
    first_one, second_one = ring_open(0, pair_one)
    third_one = ring_close(0, first_one)
    cross_two = cross(1, pair_two, second_two, third_two)
    prep_c(0)
    grad_in = nn(wc[0], gt[...]) + q[1].astype(F32)
    cross_one = cross(0, pair_one, second_one, third_one)
    near_two = send_near(1, cross_two)
    for j in range(2):
        dx_ref[j * B : (j + 1) * B, :] = grad_in[:, j * B : (j + 1) * B].T.astype(BF)
    near_one = send_near(0, cross_one)
    pl.semaphore_wait(hello.at[4], 2)
    far_two = send_far(1, near_two)
    far_one = send_far(0, near_one)
    last_two = send_last(1, far_two)
    last_one = send_last(0, far_one)
    finish(1, last_two)
    finish(0, last_one)
    for w in (pair_two, first_two, second_two, third_two, cross_two, near_two):
        pending += w
    for w in (pair_one, first_one, second_one, third_one, cross_one, near_one):
        pending += w
    pending += far_two + far_one + last_two + last_one
    for c in pending:
        c.wait_send()


def settle(*refs):
    sem = refs[8]
    copies = [pltpu.make_async_copy(refs[i], refs[4 + i], sem.at[i]) for i in range(4)]
    for c in copies:
        c.start()
    for c in copies:
        c.wait()


def on_device(n_grp, n_tile, features, source_rows, target_codes, block_count, w1, w2, cot):
    kvol, _, B = source_rows.shape
    side = math.isqrt(n_grp)
    zside = math.isqrt(n_tile // 2)
    shard = kvol * B // n_grp
    half = -(-shard // 32) * 16
    wide = kvol * B
    vmem = pl.BlockSpec(memory_space=pltpu.VMEM)
    hbm = pl.BlockSpec(memory_space=pltpu.HBM)
    dma = pltpu.SemaphoreType.DMA
    dims = (n_grp, n_tile, kvol, B, side, zside)
    held = functools.partial(
        pltpu.with_memory_space_constraint, memory_space=pltpu.HBM
    )
    results = pl.pallas_call(
        functools.partial(kernel, dims),
        out_shape=(
            jax.ShapeDtypeStruct((2 * B, B), BF),
            jax.ShapeDtypeStruct((2 * B, B), BF),
            jax.ShapeDtypeStruct((shard, B), F32),
            jax.ShapeDtypeStruct((shard, B), F32),
        ),
        in_specs=[hbm] * 7,
        out_specs=(vmem,) * 4,
        scratch_shapes=[
            pltpu.VMEM((2 * B, B), BF),
            pltpu.VMEM((kvol, 2, B), I32),
            pltpu.SMEM((2, kvol), I32),
            pltpu.SMEM((1,), I32),
            pltpu.VMEM((2 * B, B), BF),
            pltpu.VMEM((kvol, 2 * B, 2 * B), BF),
            pltpu.VMEM((5 * (kvol // 3) * B, 2 * B), BF),
            pltpu.VMEM((wide, 2 * B), BF),
            pltpu.VMEM((2, kvol, B, B), BF),
            pltpu.VMEM((2, B, wide), BF),
            pltpu.VMEM((2, B, wide), BF),
            pltpu.VMEM((B, 2 * B), BF),
            pltpu.VMEM((B, 2 * B), BF),
            pltpu.VMEM((B, 2 * B), F32),
            pltpu.VMEM((2, B, 2 * B), BF),
            pltpu.VMEM((2, 2, B, 2 * B), BF),
            pltpu.VMEM((4, 2, B, 2 * B), BF),
            pltpu.VMEM((2, B, 2 * B), BF),
            pltpu.VMEM((B, B), BF),
            pltpu.VMEM((2, wide + 2 * half - shard, B), F32),
            pltpu.VMEM((2, side, side, half, B), BF),
            pltpu.VMEM((2, side, side, half, B), BF),
            pltpu.VMEM((2, side, side, half, B), BF),
            pltpu.VMEM((2, 2, side // 2, half, B), BF),
            pltpu.VMEM((2, 2, side // 2, half, B), BF),
            pltpu.VMEM((2, 2, side // 2, half, B), BF),
            pltpu.VMEM((2, 2, side // 2, half, B), BF),
            pltpu.VMEM((2, side, half, B), BF),
            pltpu.VMEM((2, side, half, B), BF),
            pltpu.VMEM((2, zside, half, B), BF),
            pltpu.VMEM((2, zside, half, B), BF),
            pltpu.VMEM((2, 2, half, B), F32),
            dma((2,)),
            dma((5,)),
            dma((4, 2)),
            dma((4, 2)),
            dma((2, 3)),
            dma((2, 3)),
            dma((2, 2, 6)),
            dma((2, 2, 6)),
            dma((2, 2, side)),
            dma((2, 2, side)),
            dma((2, zside)),
            dma((2, zside)),
            dma((2, zside)),
            dma((2, zside)),
            dma((2,)),
            dma((2,)),
            pltpu.SemaphoreType.REGULAR((5,)),
        ],
        compiler_params=pltpu.CompilerParams(
            collective_id=0, has_side_effects=True, vmem_limit_bytes=48 * 1024 * 1024
        ),
    )(
        held(features),
        held(source_rows),
        held(target_codes.T),
        block_count,
        held(w1),
        held(w2),
        held(cot),
    )
    return pl.pallas_call(
        settle,
        out_shape=tuple(jax.ShapeDtypeStruct(r.shape, r.dtype) for r in results),
        in_specs=[vmem] * 4,
        out_specs=(hbm,) * 4,
        scratch_shapes=[dma((4,))],
        compiler_params=pltpu.CompilerParams(vmem_limit_bytes=4 * 1024 * 1024),
    )(*results)


def solution(mesh):
    n_grp, n_tile = mesh.shape["grp"], mesh.shape["tile"]
    rows = P(("grp", "tile"), None)
    return jax.shard_map(
        functools.partial(on_device, n_grp, n_tile),
        mesh=mesh,
        in_specs=(
            rows,
            P(None, ("grp", "tile"), None),
            P(None, ("grp", "tile")),
            P(("grp", "tile")),
            P(),
            P(),
            rows,
        ),
        out_specs=(rows, rows, P("grp", None), P("grp", None)),
        check_vma=False,
    )
```
